32 devices in a mesh: groups: 2 (over x), tm: 8 (over z, y), rep: 2 (over core).
Axes of the slice: x: 2, y: 2, z: 4, core: 2. Of those that a mesh axis runs over, the one named last changes fastest.
Arguments:
- signal: bfloat16 [32768, 1024], P(('groups', 'tm')), parts along dimension 0, may hold values from -6 to 6
- embed_weight: bfloat16 [1024, 512], P('rep'), may hold values from -0.1875 to 0.1875
- norm_gain: float32 [512], replicated, may hold values from 0.5 to 1.5
- qkv_weight: bfloat16 [512, 3, 512], P(None, None, 'rep'), may hold values from -0.25 to 0.25
- conv_weight: float32 [4, 3, 512], P(None, None, 'rep'), may hold values from -1.5 to 1.5
- feature_weight: bfloat16 [8, 64, 128], P('rep'), may hold values from -2.5 to 2.5
- out_weight: bfloat16 [512, 512], P('rep'), may hold values from -0.25 to 0.25
Outputs:
- mixed_out: bfloat16 [32768, 512], P(('groups', 'tm', 'rep')), parts along dimension 0
The draws below stay inside these ranges and needn't reach their ends.
There are 2 independent parts, one for each index of `groups`. The reference program is written for one: setup_inputs(seed, part) draws one part's arguments, and reference() takes and returns one part's arrays. A program takes and returns all parts, laid end to end along the dimension named above; an argument that names none is the same for every part. Nothing has to cross between parts.
All inputs are finite; a program needn't handle non-finite values.
Results may differ from the reference program's by a relative error of at most 0.0085.
Values may be sent and summed in bfloat16 or wider, within the bound.
No kernel may reach another device: no remote copies, remote signals or barrier semaphores. Data moves between devices by JAX's collectives and lax.ppermute only.
A program may use at most 64 MiB of HBM per device.

```python
import jax
import jax.numpy as jnp
from jax import lax

C = 1024
H = 8
HD = 64
FEAT = 128
TAPS = 4
BLOCK = 512
D = 512
L = 16384


def level_of(key, dims, shards, smallest, high):
    factor_of = 1.0
    for axis_at, parts in shards:
        heights = jax.random.uniform(jax.random.fold_in(jax.random.fold_in(key, 6), axis_at), (parts,), jnp.float32, smallest / len(shards), high / len(shards))
        factor_of = factor_of * jnp.repeat(jnp.exp(heights), dims[axis_at] // parts).reshape((-1,) + (1,) * (len(dims) - 1 - axis_at))
    return factor_of


def gaussian(stream_key, shape, spread, bound, shards=(), dtype=jnp.bfloat16):
    drawn = jax.random.normal(stream_key, shape, jnp.float32) * spread
    if len(shards) > 0:
        drawn = level_of(stream_key, shape, shards, -0.22, 0.18) * drawn
    return jnp.clip(drawn, min=-bound, max=bound).astype(dtype)


def setup_inputs(seed: int = 0, part: int = 0) -> dict:
    key_of = jax.random.split(jax.random.key(seed), 8)
    part_keys = jax.random.split(jax.random.fold_in(key_of[7], part), 8)
    signal = gaussian(part_keys[0], (L, C), 1.0, 6.0, ((0, 8),))
    embed_weight = gaussian(key_of[1], (C, D), C ** -0.5, 0.1875, ((0, 2),))
    norm_gain = jnp.clip(1.0 + 0.1 * jax.random.normal(key_of[2], (D,), jnp.float32), 0.5, 1.5)
    qkv_weight = gaussian(key_of[3], (D, 3, D), D ** -0.5, 0.25, ((2, 2),))
    conv_weight = gaussian(key_of[4], (TAPS, 3, D), 0.5, 1.5, ((2, 2),), jnp.float32)
    feature_weight = gaussian(key_of[5], (H, HD, FEAT), 1.0, 2.5, ((0, 2),))
    out_weight = gaussian(key_of[6], (D, D), D ** -0.5, 0.25, ((0, 2),))
    return {"signal": signal, "embed_weight": embed_weight, "norm_gain": norm_gain, "qkv_weight": qkv_weight, "conv_weight": conv_weight, "feature_weight": feature_weight, "out_weight": out_weight}


def reference(signal, embed_weight, norm_gain, qkv_weight, conv_weight, feature_weight, out_weight):
    high = lax.Precision.HIGHEST
    length = signal.shape[0]
    embedded = jnp.dot(signal, embed_weight, preferred_element_type=jnp.float32)
    normed = (embedded * lax.rsqrt(lax.optimization_barrier(jnp.mean(embedded * embedded, -1, keepdims=True)) + 1e-05) * norm_gain).astype(jnp.bfloat16)
    projected = jnp.dot(normed, qkv_weight.reshape(D, 3 * D), preferred_element_type=jnp.float32).astype(jnp.bfloat16)
    padded = jnp.concatenate([jnp.zeros((TAPS - 1, 3 * D), jnp.bfloat16), projected], 0)
    kernel = conv_weight.reshape(TAPS, 3 * D)
    convolved = jnp.zeros((length, 3 * D), jnp.float32)
    for tap in range(TAPS):
        convolved = convolved + kernel[tap] * padded[tap:tap + length].astype(jnp.float32)
    query = convolved[:, :D].astype(jnp.bfloat16).reshape(length, H, HD)
    key = convolved[:, D:2 * D].astype(jnp.bfloat16).reshape(length, H, HD)
    value = convolved[:, 2 * D:].astype(jnp.bfloat16).reshape(length, H, HD)
    feats = feature_weight.astype(jnp.float32)

    def features(part):
        pf = part.astype(jnp.float32)
        unit = pf * lax.rsqrt(lax.optimization_barrier(jnp.mean(pf * pf, -1, keepdims=True)) + 1e-05) / jnp.sqrt(jnp.float32(HD))
        return jnp.exp(jnp.einsum('thd,hdf->thf', unit, feats, precision=high)).astype(jnp.bfloat16)
    query_feat = features(query).reshape(length // BLOCK, BLOCK, H, FEAT)
    key_feat = features(key).reshape(length // BLOCK, BLOCK, H, FEAT)
    values = value.reshape(length // BLOCK, BLOCK, H, HD)
    causal = jnp.arange(BLOCK)[:, None] >= jnp.arange(BLOCK)[None, :]

    def advance(carry, items):
        state, total = carry
        qb, kb, vb = items
        qf = qb.astype(jnp.float32)
        kf = kb.astype(jnp.float32)
        vf = vb.astype(jnp.float32)
        scores = jnp.einsum('thf,shf->hts', qf, kf, precision=high)
        weights = jnp.where(causal[None], scores, 0.0).astype(jnp.bfloat16).astype(jnp.float32)
        numer = jnp.einsum('hts,shd->thd', weights, vf, precision=high)
        numer = numer + jnp.einsum('thf,hfd->thd', qf, state, precision=high)
        denom = lax.optimization_barrier(jnp.sum(weights, -1)).T + jnp.einsum('thf,hf->th', qf, total, precision=high)
        out = (numer / denom[:, :, None]).astype(jnp.bfloat16).reshape(BLOCK, D)
        state = state + jnp.einsum('shf,shd->hfd', kf, vf, precision=high)
        total = total + lax.optimization_barrier(jnp.sum(kf, 0))
        return ((state, total), out)
    start = (jnp.zeros((H, FEAT, HD), jnp.float32), jnp.zeros((H, FEAT), jnp.float32))
    _, outs = lax.scan(advance, start, (query_feat, key_feat, values))
    attended = outs.reshape(length, D)
    return jnp.dot(attended, out_weight, preferred_element_type=jnp.float32).astype(jnp.bfloat16)
```

```python
import functools
import math

import jax
import jax.numpy as jnp
from jax import lax
from jax.experimental import pallas as pl
from jax.experimental.pallas import tpu as pltpu
from jax.sharding import PartitionSpec as P

EPS = 1e-05
LOG2E = math.log2(math.e)
SUB = 256
STEP = 512
RIM = 16
PAD = 8
LANES = 128
F32 = jnp.float32
BF16 = jnp.bfloat16
NT = (((1,), (1,)), ((), ()))
TN = (((0,), (0,)), ((), ()))


def dot(a, b, dims=(((1,), (0,)), ((), ()))):
    return lax.dot_general(a, b, dims, preferred_element_type=F32)


def params(mib=40):
    return pltpu.CompilerParams(dimension_semantics=("arbitrary",), vmem_limit_bytes=mib << 20)


def whole(shape):
    zeros = (0,) * len(shape)
    return pl.BlockSpec(shape, lambda *_: zeros)


def normalize(sig_a, sig_b, ew_a, ew_b, gain):
    emb = dot(sig_a, ew_a) + dot(sig_b, ew_b)
    mean = jnp.mean(emb * emb, -1, keepdims=True)
    return (emb * lax.rsqrt(mean + EPS) * gain).astype(BF16)


def convolve(pad_ref, proj, taps_ref, parts):
    rows = proj.shape[0]
    taps = taps_ref.shape[0]
    tiles = proj.shape[1] // LANES
    per = tiles // len(parts)
    out = []
    for c in range(tiles):
        pad_ref[c, PAD : PAD + rows, :] = proj[:, c * LANES : (c + 1) * LANES]
    for c in range(tiles):
        at = (c % per) * LANES
        total = None
        for tap in range(taps):
            weight = taps_ref[tap, parts[c // per] : parts[c // per] + 1, at : at + LANES]
            term = weight * pad_ref[c, PAD - taps + 1 + tap : PAD - taps + 1 + tap + rows, :]
            total = term if total is None else total + term
        out.append(total.astype(BF16))
    for c in range(tiles):
        pad_ref[c, 0:PAD, :] = pad_ref[c, rows : rows + PAD, :]
    return out


def start_rim(pad_ref, proj, keep):
    rows = proj.shape[0]
    for c in range(pad_ref.shape[0]):
        pad_ref[c, 0:PAD, :] = proj[rows - PAD :, c * LANES : (c + 1) * LANES] * keep


def spread_features(feat_ref, diag_ref, ones_ref):
    heads, head_dim, feat = feat_ref.shape
    diag_ref[...] = jnp.zeros_like(diag_ref)
    ones_ref[...] = jnp.zeros_like(ones_ref)
    for h in range(heads):
        at = (slice(h * head_dim, (h + 1) * head_dim), slice(h * feat, (h + 1) * feat))
        diag_ref[at] = feat_ref[h]
        ones_ref[at] = jnp.ones((head_dim, feat), BF16)


def features(part, diag_ref, ones_ref, head_dim):
    part_f = part.astype(F32)
    logits = dot(part, diag_ref[...])
    squares = dot((part_f * part_f).astype(BF16), ones_ref[...])
    scale = lax.rsqrt(squares * (1.0 / head_dim) + EPS) * (LOG2E / math.sqrt(head_dim))
    return jnp.exp2(logits * scale).astype(BF16)


def key_kernel(
    sc, sig_a, sig_b, rim_a, rim_b, ew_a, ew_b, gain, weight, taps, feat_w,
    normed_ref, nrim_ref, kf_ref, v_ref, before_ref, total_ref,
    pad, diag, ones, acc,
):
    step = pl.program_id(0)
    cols = v_ref.shape[1]
    heads, head_dim, feat = feat_w.shape

    @pl.when(step == 0)
    def _():
        spread_features(feat_w, diag, ones)
        nrim = normalize(rim_a[...], rim_b[...], ew_a[...], ew_b[...], gain[...])
        nrim_ref[...] = nrim
        keep = (sc[1] > 0).astype(F32)
        proj = dot(nrim, weight[:, cols:]).astype(BF16).astype(F32)
        start_rim(pad, proj, keep)
        acc[...] = jnp.zeros_like(acc)

    normed = normalize(sig_a[...], sig_b[...], ew_a[...], ew_b[...], gain[...])
    normed_ref[...] = normed
    proj = dot(normed, weight[:, cols:]).astype(BF16).astype(F32)
    tiles = convolve(pad, proj, taps, (1, 2))
    half = len(tiles) // 2
    key = jnp.concatenate(tiles[:half], 1)
    value = jnp.concatenate(tiles[half:], 1)
    v_ref[...] = value
    key_feat = features(key, diag, ones, head_dim)
    kf_ref[...] = key_feat
    for b in range(key.shape[0] // SUB):
        rows = slice(b * SUB, (b + 1) * SUB)
        before_ref[b] = acc[...]
        for pair in range(heads // 2):
            vp = value[rows, pair * 2 * head_dim : (pair + 1) * 2 * head_dim]
            kp = key_feat[rows, pair * 2 * feat : (pair + 1) * 2 * feat]
            both = dot(vp, kp, TN)
            for side in range(2):
                h = pair * 2 + side
                acc[h * head_dim : (h + 1) * head_dim, :] += both[
                    side * head_dim : (side + 1) * head_dim, side * feat : (side + 1) * feat
                ]
        sums = jnp.sum(key_feat[rows].astype(F32), 0, keepdims=True)
        for h in range(heads):
            at = heads * head_dim + h
            acc[at : at + 1, :] += sums[:, h * feat : (h + 1) * feat]

    @pl.when(step == pl.num_programs(0) - 1)
    def _():
        total_ref[...] = acc[...].astype(BF16)


def query_kernel(sc, normed, nrim, weight, taps, feat_w, qf_ref, pad, diag, ones):
    cols = weight.shape[1] // 3

    @pl.when(pl.program_id(0) == 0)
    def _():
        spread_features(feat_w, diag, ones)
        keep = (sc[1] > 0).astype(F32)
        start_rim(pad, dot(nrim[...], weight[:, :cols]).astype(BF16).astype(F32), keep)

    proj = dot(normed[...], weight[:, :cols]).astype(BF16).astype(F32)
    query = jnp.concatenate(convolve(pad, proj, taps, (0,)), 1)
    qf_ref[...] = features(query, diag, ones, feat_w.shape[1])


def local_kernel(qf, kf, v, out_ref, *, heads):
    feat = qf.shape[1] // heads
    width = v.shape[1] // heads
    row = lax.broadcasted_iota(jnp.int32, (SUB, SUB), 0)
    col = lax.broadcasted_iota(jnp.int32, (SUB, SUB), 1)
    causal = row >= col
    left = lax.broadcasted_iota(jnp.int32, (SUB, 2 * width), 1) < width
    one, zero = jnp.ones((SUB, 2 * width), BF16), jnp.zeros((SUB, 2 * width), BF16)
    for b in range(qf.shape[0] // SUB):
        rows = slice(b * SUB, (b + 1) * SUB)
        for pair in range(heads // 2):
            vp = v[rows, pair * 2 * width : (pair + 1) * 2 * width]
            total = None
            for side in range(2):
                at = slice((pair * 2 + side) * feat, (pair * 2 + side + 1) * feat)
                mine = left if side == 0 else ~left
                scores = dot(qf[rows, at], kf[rows, at], NT)
                weights = jnp.where(causal, scores, 0.0).astype(BF16)
                rhs = jnp.concatenate([jnp.where(mine, vp, zero), jnp.where(mine, one, zero)], 1)
                term = dot(weights, rhs)
                total = term if total is None else total + term
            out_ref[rows, pair * 4 * width : (pair + 1) * 4 * width] = total


def combine_kernel(sc, qf, local, before, near, far, out_ref, *, heads):
    feat = qf.shape[1] // heads
    width = out_ref.shape[1] // heads
    state_in = near[...] + far[...].astype(F32) * (sc[2] > 0).astype(F32)
    zero = jnp.zeros((width, feat), BF16)
    for b in range(qf.shape[0] // SUB):
        rows = slice(b * SUB, (b + 1) * SUB)
        state = (before[b] + state_in).astype(BF16)
        for pair in range(heads // 2):
            h = pair * 2
            s0, s1 = (state[(h + k) * width : (h + k + 1) * width] for k in range(2))
            t0, t1 = (
                jnp.broadcast_to(
                    state[heads * width + h + k : heads * width + h + k + 1], (width, feat)
                )
                for k in range(2)
            )
            rhs = jnp.concatenate(
                [
                    jnp.concatenate([s0, zero], 1),
                    jnp.concatenate([zero, s1], 1),
                    jnp.concatenate([t0, zero], 1),
                    jnp.concatenate([zero, t1], 1),
                ],
                0,
            )
            both = local[rows, pair * 4 * width : (pair + 1) * 4 * width] + dot(
                qf[rows, pair * 2 * feat : (pair + 1) * 2 * feat], rhs, NT
            )
            out_ref[rows, pair * 2 * width : (pair + 1) * 2 * width] = (
                both[:, : 2 * width] / both[:, 2 * width :]
            ).astype(BF16)


def output_kernel(mine, other, w_mine, w_other, out_ref):
    out_ref[...] = (dot(mine[...], w_mine[...]) + dot(other[...], w_other[...])).astype(BF16)


def swap(array, axis, by):
    devices = lax.axis_size(axis)
    return lax.ppermute(array, axis, [(i, i ^ by) for i in range(devices)])


def prefix(total, axis):
    devices = lax.axis_size(axis)
    place = lax.axis_index(axis)
    near = jnp.zeros(total.shape, F32)
    group = total.astype(F32)
    span = 1
    while True:
        radix = min(4, devices // span)
        sent = group.astype(BF16)
        got = [swap(sent, axis, k * span) for k in range(1, radix)]
        if span * radix >= devices and radix == 2:
            return near, got[0], (place & span) > 0
        digit = (place // span) % radix
        for k, g in enumerate(got, 1):
            g = g.astype(F32)
            group = group + g
            near = near + jnp.where((digit ^ k) < digit, g, 0.0)
        span *= radix
        if span >= devices:
            return near, jnp.zeros_like(total), place < 0


def shards(signal, embed_weight, norm_gain, qkv_weight, conv_weight, feature_weight, out_weight):
    rows, depth = signal.shape
    half_depth, width = embed_weight.shape
    cols = qkv_weight.shape[2]
    heads, head_dim, feat = feature_weight.shape
    feats = heads * feat
    states = heads * head_dim + 16
    taps = conv_weight.shape[0]
    place, rep = lax.axis_index("tm"), lax.axis_index("rep")
    devices = lax.axis_size("tm")

    ew_other = swap(embed_weight, "rep", 1)
    rim = lax.ppermute(signal[rows - RIM :], "tm", [(i, (i + 1) % devices) for i in range(devices)])
    ow_other = swap(out_weight, "rep", 1)
    weight = qkv_weight.reshape(width, 3 * cols)
    sc = jnp.stack([rep, place]).astype(jnp.int32)
    gain = norm_gain.reshape(1, width)
    steps = rows // STEP
    scratch = [
        pltpu.VMEM((2 * cols // LANES, PAD + STEP, LANES), F32),
        pltpu.VMEM((cols, feats), BF16),
        pltpu.VMEM((cols, feats), BF16),
        pltpu.VMEM((states, feat), F32),
    ]
    normed, nrim, kf, value, before, total = pl.pallas_call(
        key_kernel,
        grid_spec=pltpu.PrefetchScalarGridSpec(
            num_scalar_prefetch=1,
            grid=(steps,),
            in_specs=[
                pl.BlockSpec((STEP, half_depth), lambda i, s: (i, s[0])),
                pl.BlockSpec((STEP, half_depth), lambda i, s: (i, 1 - s[0])),
                pl.BlockSpec((RIM, half_depth), lambda i, s: (0, s[0])),
                pl.BlockSpec((RIM, half_depth), lambda i, s: (0, 1 - s[0])),
                whole((half_depth, width)),
                whole((half_depth, width)),
                whole((1, width)),
                whole((width, 3 * cols)),
                whole(conv_weight.shape),
                whole(feature_weight.shape),
            ],
            out_specs=[
                pl.BlockSpec((STEP, width), lambda i, s: (i, 0)),
                whole((RIM, width)),
                pl.BlockSpec((STEP, feats), lambda i, s: (i, 0)),
                pl.BlockSpec((STEP, cols), lambda i, s: (i, 0)),
                pl.BlockSpec((STEP // SUB, states, feat), lambda i, s: (i, 0, 0)),
                whole((states, feat)),
            ],
            scratch_shapes=scratch,
        ),
        out_shape=[
            jax.ShapeDtypeStruct((rows, width), BF16),
            jax.ShapeDtypeStruct((RIM, width), BF16),
            jax.ShapeDtypeStruct((rows, feats), BF16),
            jax.ShapeDtypeStruct((rows, cols), BF16),
            jax.ShapeDtypeStruct((rows // SUB, states, feat), F32),
            jax.ShapeDtypeStruct((states, feat), BF16),
        ],
        compiler_params=params(),
        name="keys",
    )(sc, signal, signal, rim, rim, embed_weight, ew_other, gain, weight, conv_weight, feature_weight)

    near, far, flag = prefix(total, "tm")

    query_feat = pl.pallas_call(
        query_kernel,
        grid_spec=pltpu.PrefetchScalarGridSpec(
            num_scalar_prefetch=1,
            grid=(steps,),
            in_specs=[
                pl.BlockSpec((STEP, width), lambda i, s: (i, 0)),
                whole((RIM, width)),
                whole((width, 3 * cols)),
                whole(conv_weight.shape),
                whole(feature_weight.shape),
            ],
            out_specs=pl.BlockSpec((STEP, feats), lambda i, s: (i, 0)),
            scratch_shapes=[
                pltpu.VMEM((cols // LANES, PAD + STEP, LANES), F32),
                pltpu.VMEM((cols, feats), BF16),
                pltpu.VMEM((cols, feats), BF16),
            ],
        ),
        out_shape=jax.ShapeDtypeStruct((rows, feats), BF16),
        compiler_params=params(),
        cost_estimate=pl.CostEstimate(flops=2 * rows * width * cols * 4, bytes_accessed=8 << 20, transcendentals=0),
        name="queries",
    )(sc, normed, nrim, weight, conv_weight, feature_weight)

    local = pl.pallas_call(
        functools.partial(local_kernel, heads=heads),
        grid=(steps,),
        in_specs=[
            pl.BlockSpec((STEP, feats), lambda i: (i, 0)),
            pl.BlockSpec((STEP, feats), lambda i: (i, 0)),
            pl.BlockSpec((STEP, cols), lambda i: (i, 0)),
        ],
        out_specs=pl.BlockSpec((STEP, 2 * cols), lambda i: (i, 0)),
        out_shape=jax.ShapeDtypeStruct((rows, 2 * cols), F32),
        compiler_params=params(),
        cost_estimate=pl.CostEstimate(flops=2 * rows * SUB * 1024 * 4, bytes_accessed=9 << 20, transcendentals=0),
        name="local",
    )(query_feat, kf, value)

    half = rows // 2
    half_steps = half // STEP

    def combine(which):
        scal = jnp.stack([which * half_steps, which, flag]).astype(jnp.int32)
        return pl.pallas_call(
            functools.partial(combine_kernel, heads=heads),
            grid_spec=pltpu.PrefetchScalarGridSpec(
                num_scalar_prefetch=1,
                grid=(half_steps,),
                in_specs=[
                    pl.BlockSpec((STEP, feats), lambda i, s: (i + s[0], 0)),
                    pl.BlockSpec((STEP, 2 * cols), lambda i, s: (i + s[0], 0)),
                    pl.BlockSpec((STEP // SUB, states, feat), lambda i, s: (i + s[0], 0, 0)),
                    whole((states, feat)),
                    whole((states, feat)),
                ],
                out_specs=pl.BlockSpec((STEP, cols), lambda i, s: (i, 0)),
            ),
            out_shape=jax.ShapeDtypeStruct((half, cols), BF16),
            compiler_params=params(),
            cost_estimate=pl.CostEstimate(flops=2 * half * 256 * 512, bytes_accessed=4 << 20, transcendentals=0),
            name="combine",
        )(scal, query_feat, local, before, near, far)

    for_other = swap(combine(1 - rep), "rep", 1)
    mine = combine(rep)
    return pl.pallas_call(
        output_kernel,
        grid=(half_steps,),
        in_specs=[
            pl.BlockSpec((STEP, cols), lambda i: (i, 0)),
            pl.BlockSpec((STEP, cols), lambda i: (i, 0)),
            whole(out_weight.shape),
            whole(out_weight.shape),
        ],
        out_specs=pl.BlockSpec((STEP, width), lambda i: (i, 0)),
        out_shape=jax.ShapeDtypeStruct((half, width), BF16),
        compiler_params=params(),
        name="output",
    )(mine, for_other, out_weight, ow_other)


def solution(mesh):
    in_specs = (
        P(("groups", "tm"), None),
        P("rep", None),
        P(),
        P(None, None, "rep"),
        P(None, None, "rep"),
        P("rep", None, None),
        P("rep", None),
    )
    out_specs = P(("groups", "tm", "rep"), None)
    return jax.shard_map(shards, mesh=mesh, in_specs=in_specs, out_specs=out_specs, check_vma=False)
```

```python
import functools
import math

import jax
import jax.numpy as jnp
from jax import lax
from jax.experimental import pallas as pl
from jax.experimental.pallas import tpu as pltpu
from jax.sharding import PartitionSpec as P

EPS = 1e-05
LOG2E = math.log2(math.e)
SUB = 256
RIM = 16
PAD = 8
LANES = 128
F32 = jnp.float32
BF16 = jnp.bfloat16
NN = (((1,), (0,)), ((), ()))
NT = (((1,), (1,)), ((), ()))
TN = (((0,), (0,)), ((), ()))


def dot(a, b, dims=NN):
    return lax.dot_general(a, b, dims, preferred_element_type=F32)


def call(kernel, ins, outs, name, scratch=(), work=(1, 1), mib=16):
    def spec(place):
        return pl.BlockSpec(memory_space=pltpu.VMEM if place is None else place)

    def pinned(array, place):
        return pltpu.with_memory_space_constraint(array, place) if place is pltpu.HBM else array

    return pl.pallas_call(
        kernel,
        in_specs=[spec(p) for _, p in ins],
        out_specs=[spec(p) for _, _, p in outs],
        out_shape=[jax.ShapeDtypeStruct(s, t) for s, t, _ in outs],
        scratch_shapes=list(scratch),
        compiler_params=pltpu.CompilerParams(vmem_limit_bytes=mib << 20),
        cost_estimate=pl.CostEstimate(flops=work[0] << 3, bytes_accessed=work[1], transcendentals=0),
        name=name,
    )(*[pinned(*i) for i in ins])


def vmem(*arrays):
    return [(a, None) for a in arrays]


def normalize(emb, gain):
    mean = jnp.mean(emb * emb, -1, keepdims=True)
    return (emb * lax.rsqrt(mean + EPS) * gain).astype(BF16)


def embed_own_kernel(
    sc, sig, ew_hbm, gain_hbm,
    partial, sig_other, near_rim, far_rim, ew, gain,
    buf, sem, late_sem,
):
    rep = sc[0]
    rows, half = sig_other.shape
    blocks = rows // SUB
    own = pl.ds(pl.multiple_of(rep * half, half), half)
    other = pl.ds(pl.multiple_of((1 - rep) * half, half), half)
    weight = pltpu.make_async_copy(ew_hbm, ew, late_sem.at[0])
    weight.start()
    copies = []
    for b in range(blocks):
        at = pl.ds(pl.multiple_of(rep * rows + b * SUB, SUB), SUB)
        copies.append(pltpu.make_async_copy(sig.at[at, own], buf.at[b], sem.at[b]))
        copies[-1].start()
    all_rows = pl.ds(pl.multiple_of(rep * rows, SUB), rows)
    late = [
        pltpu.make_async_copy(sig.at[pl.ds(2 * rows - RIM, RIM), :], far_rim, late_sem.at[1]),
        pltpu.make_async_copy(sig.at[pl.ds(rows - RIM, RIM), :], near_rim, late_sem.at[2]),
        pltpu.make_async_copy(gain_hbm, gain, late_sem.at[3]),
        pltpu.make_async_copy(sig.at[all_rows, other], sig_other, late_sem.at[4]),
    ]
    for copy in late:
        copy.start()
    weight.wait()
    for b in range(blocks):
        copies[b].wait()
        partial[b * SUB : (b + 1) * SUB, :] = dot(buf[b], ew[...])
    for copy in late:
        copy.wait()


def embed_other_kernel(partial, sig_other, ew_own, ew, gain, normed, ew_on):
    ew_on[...] = ew_own[...]
    for b in range(normed.shape[0] // SUB):
        rows = slice(b * SUB, (b + 1) * SUB)
        normed[rows, :] = normalize(partial[rows, :] + dot(sig_other[rows, :], ew[...]), gain[...])


def store_proj(pad, normed, weights, start):
    rows = normed.shape[0]
    c = 0
    for w in weights:
        proj = dot(normed, w).astype(BF16).astype(F32)
        for j in range(w.shape[1] // LANES):
            pad[c, start : start + rows, :] = proj[:, j * LANES : (j + 1) * LANES]
            c += 1


def convolve(pad, taps, part, first, count, start, rows):
    out = []
    for j in range(count):
        total = None
        for tap in range(taps.shape[1]):
            at = start - taps.shape[1] + 1 + tap
            weight = taps[part, tap : tap + 1, j * LANES : (j + 1) * LANES]
            term = weight * pad[first + j, at : at + rows, :]
            total = term if total is None else total + term
        out.append(total.astype(BF16))
    return jnp.concatenate(out, 1)


def features(part, diag, ones, head_dim):
    part_f = part.astype(F32)
    logits = dot(part, diag[...])
    squares = dot((part_f * part_f).astype(BF16), ones[...])
    scale = lax.rsqrt(squares * (1.0 / head_dim) + EPS) * (LOG2E / math.sqrt(head_dim))
    return jnp.exp2(logits * scale).astype(BF16)


def rim_rows(pad, nrim, weights, keep):
    c = 0
    for w in weights:
        proj = dot(nrim, w).astype(BF16).astype(F32) * keep
        for j in range(w.shape[1] // LANES):
            pad[c, 0:PAD, :] = proj[RIM - PAD :, j * LANES : (j + 1) * LANES]
            c += 1


def key_body(sc, normed, nrim, weight, taps, feat_w, kf, val, before, total, diag, ones, pad):
    heads, head_dim, feat = feat_w.shape
    cols = val.shape[1]
    tiles = cols // LANES
    diag[...] = jnp.zeros_like(diag)
    ones[...] = jnp.zeros_like(ones)
    for h in range(heads):
        at = (slice(h * head_dim, (h + 1) * head_dim), slice(h * feat, (h + 1) * feat))
        diag[at] = feat_w[h]
        ones[at] = jnp.ones((head_dim, feat), BF16)
    weights = (weight[1], weight[2])
    rim_rows(pad, nrim, weights, (sc[1] > 0).astype(F32))
    total[...] = jnp.zeros_like(total)
    for b in range(normed.shape[0] // SUB):
        rows = slice(b * SUB, (b + 1) * SUB)
        start = PAD + b * SUB
        store_proj(pad, normed[rows, :], weights, start)
        key = convolve(pad, taps, 1, 0, tiles, start, SUB)
        value = convolve(pad, taps, 2, tiles, tiles, start, SUB)
        val[rows, :] = value
        key_feat = features(key, diag, ones, head_dim)
        kf[rows, :] = key_feat
        before[b] = total[...]
        for pair in range(heads // 2):
            vp = value[:, pair * 2 * head_dim : (pair + 1) * 2 * head_dim]
            kp = key_feat[:, pair * 2 * feat : (pair + 1) * 2 * feat]
            both = dot(vp, kp, TN)
            for side in range(2):
                h = pair * 2 + side
                total[h * head_dim : (h + 1) * head_dim, :] += both[
                    side * head_dim : (side + 1) * head_dim, side * feat : (side + 1) * feat
                ]
        sums = jnp.sum(key_feat.astype(F32), 0, keepdims=True)
        for h in range(heads):
            at = heads * head_dim + h
            total[at : at + 1, :] += sums[:, h * feat : (h + 1) * feat]


def first_key_kernel(
    sc, far_rim, near_rim, ew_a, ew_b, gain, normed, weight, taps, feat_w,
    nrim, kf, val, before, total, diag, ones, pad,
):
    half = ew_a.shape[0]
    own = sc[0] == 0
    rim = jnp.where(own, far_rim[...].astype(F32), near_rim[...].astype(F32))
    lo, hi = rim[:, :half], rim[:, half:]
    mine = jnp.where(own, lo, hi).astype(BF16)
    other = jnp.where(own, hi, lo).astype(BF16)
    rows_n = normalize(dot(mine, ew_a[...]) + dot(other, ew_b[...]), gain[...])
    nrim[...] = rows_n
    key_body(sc, normed, rows_n, weight, taps, feat_w, kf, val, before, total, diag, ones, pad)


def key_kernel(
    sc, normed, nrim, weight, taps, feat_w, ow_hbm,
    kf, val, before, total, diag, ones, ow, pad, sem,
):
    copy = pltpu.make_async_copy(ow_hbm, ow, sem)
    copy.start()
    key_body(sc, normed, nrim[...], weight, taps, feat_w, kf, val, before, total, diag, ones, pad)
    copy.wait()


def query_kernel(
    sc, after, normed, nrim, weight, taps, diag, ones, kf, val, qf, out, pad, *, heads
):
    del after
    tiles = weight.shape[2] // LANES
    feat = qf.shape[1] // heads
    width = val.shape[1] // heads
    row = lax.broadcasted_iota(jnp.int32, (SUB, SUB), 0)
    col = lax.broadcasted_iota(jnp.int32, (SUB, SUB), 1)
    causal = row >= col
    left = lax.broadcasted_iota(jnp.int32, (SUB, 2 * width), 1) < width
    one, zero = jnp.ones((SUB, 2 * width), BF16), jnp.zeros((SUB, 2 * width), BF16)
    rim_rows(pad, nrim[...], (weight[0],), (sc[1] > 0).astype(F32))
    for b in range(normed.shape[0] // SUB):
        rows = slice(b * SUB, (b + 1) * SUB)
        start = PAD + b * SUB
        store_proj(pad, normed[rows, :], (weight[0],), start)
        query = convolve(pad, taps, 0, 0, tiles, start, SUB)
        query_feat = features(query, diag, ones, width)
        qf[rows, :] = query_feat
        for pair in range(heads // 2):
            vp = val[rows, pair * 2 * width : (pair + 1) * 2 * width]
            total = None
            for side in range(2):
                at = slice((pair * 2 + side) * feat, (pair * 2 + side + 1) * feat)
                mine = left if side == 0 else ~left
                scores = dot(query_feat[:, at], kf[rows, at], NT)
                weights = jnp.where(causal, scores, 0.0).astype(BF16)
                rhs = jnp.concatenate([jnp.where(mine, vp, zero), jnp.where(mine, one, zero)], 1)
                term = dot(weights, rhs)
                total = term if total is None else total + term
            out[rows, pair * 4 * width : (pair + 1) * 4 * width] = total


def attend(qf, local, before, state_in, b, heads):
    feat = qf.shape[1] // heads
    width = local.shape[1] // heads // 2
    zero = jnp.zeros((width, feat), BF16)
    rows = slice(b * SUB, (b + 1) * SUB)
    state = (before[b] + state_in).astype(BF16)
    out = []
    for pair in range(heads // 2):
        h = pair * 2
        s0, s1 = (state[(h + k) * width : (h + k + 1) * width] for k in range(2))
        t0, t1 = (
            jnp.broadcast_to(
                state[heads * width + h + k : heads * width + h + k + 1], (width, feat)
            )
            for k in range(2)
        )
        rhs = jnp.concatenate(
            [
                jnp.concatenate([s0, zero], 1),
                jnp.concatenate([zero, s1], 1),
                jnp.concatenate([t0, zero], 1),
                jnp.concatenate([zero, t1], 1),
            ],
            0,
        )
        both = local[rows, pair * 4 * width : (pair + 1) * 4 * width] + dot(
            qf[rows, pair * 2 * feat : (pair + 1) * 2 * feat], rhs, NT
        )
        out.append((both[:, : 2 * width] / both[:, 2 * width :]).astype(BF16))
    return jnp.concatenate(out, 1)


def own_kernel(qf, local, before, state, weight, out, *, heads):
    for b in range(qf.shape[0] // SUB):
        out[b * SUB : (b + 1) * SUB, :] = dot(
            attend(qf, local, before, state[...], b, heads), weight[...]
        )


def last_kernel(qf, local, before, state, weight, partial, out, buf, sem, *, heads):
    copies = []
    for b in range(qf.shape[0] // SUB):
        rows = slice(b * SUB, (b + 1) * SUB)
        attended = attend(qf, local, before, state[...].astype(F32), b, heads)
        buf[b] = (partial[rows, :] + dot(attended, weight[...])).astype(BF16)
        copies.append(pltpu.make_async_copy(buf.at[b], out.at[pl.ds(b * SUB, SUB), :], sem.at[b]))
        copies[-1].start()
    for copy in copies:
        copy.wait()


def swap(array, axis, by):
    devices = lax.axis_size(axis)
    return lax.ppermute(array, axis, [(i, i ^ by) for i in range(devices)])


def rounds(axis):
    devices, span, out = lax.axis_size(axis), 1, []
    while span < devices:
        radix = min(4, devices // span)
        out.append((span, radix))
        span *= radix
    return out


def earlier(axis):
    place = lax.axis_index(axis)
    flags = []
    for span, radix in rounds(axis):
        digit = (place >> (span.bit_length() - 1)) & (radix - 1)
        flags += [(digit ^ k) < digit for k in range(1, radix)]
    return flags


def prefix(group, axis, masks, covers):
    near = jnp.zeros(group.shape, F32)
    row = 0
    for span, radix in rounds(axis):
        sent = group.astype(BF16)
        if covers:
            covers.pop(0)(sent)
        for k in range(1, radix):
            got = swap(sent, axis, k * span).astype(F32)
            group = group + got
            near = near + jnp.where(masks[row : row + 1] > 0, got, 0.0)
            row += 1
    while covers:
        covers.pop(0)(group)
    return near


def shards(signal, embed_weight, norm_gain, qkv_weight, conv_weight, feature_weight, out_weight):
    rows, depth = signal.shape
    rows //= 2
    half, width = embed_weight.shape
    cols = qkv_weight.shape[2]
    heads, head_dim, feat = feature_weight.shape
    feats = heads * feat
    states = heads * head_dim + 16
    blocks = rows // SUB
    place, rep = lax.axis_index("tm"), lax.axis_index("rep")
    devices = lax.axis_size("tm")
    smem, hbm = pltpu.SMEM, pltpu.HBM

    ew_other = swap(embed_weight, "rep", 1)
    wqkv = [qkv_weight.transpose(1, 0, 2), swap(qkv_weight.transpose(1, 0, 2), "rep", 1)]
    taps = [conv_weight.transpose(1, 0, 2), swap(conv_weight.transpose(1, 0, 2), "rep", 1)]
    feat_w = [feature_weight, swap(feature_weight, "rep", 1)]
    sc = jnp.stack([rep, 2 * place + rep]).astype(jnp.int32)
    flags = jnp.stack([rep > 0, *earlier("tm")]).astype(F32)
    sc, masks = lax.optimization_barrier((sc, jnp.broadcast_to(flags[:, None], (flags.size, feat))))
    second, masks = masks[:1] > 0, masks[1:]
    gain = norm_gain.reshape(1, width)

    partial, sig_other, near_rim, _, ew_own, gain = call(
        embed_own_kernel,
        [(sc, smem), (signal, hbm), (embed_weight, hbm), (gain, hbm)],
        [
            ((rows, width), F32, None),
            ((rows, half), BF16, None),
            ((RIM, depth), BF16, None),
            ((RIM, depth), BF16, None),
            ((half, width), BF16, None),
            ((1, width), F32, None),
        ],
        "embed_own",
        [
            pltpu.VMEM((blocks, SUB, half), BF16),
            pltpu.SemaphoreType.DMA((blocks,)),
            pltpu.SemaphoreType.DMA((5,)),
        ],
        (2 * rows * half * width, 4 << 20),
    )
    far_rim = lax.ppermute(signal[2 * rows - RIM :], "tm", [(i, (i + 1) % devices) for i in range(devices)])
    normed, ew_own = call(
        embed_other_kernel,
        vmem(partial, sig_other, ew_own, ew_other, gain),
        [((rows, width), BF16, None), ((half, width), BF16, None)],
        "embed_other",
        (),
        (8, 8),
    )

    key_outs = [
        ((rows, feats), BF16, None),
        ((rows, cols), BF16, None),
        ((blocks, states, feat), F32, None),
        ((states, feat), F32, None),
        ((cols, feats), BF16, None),
        ((cols, feats), BF16, None),
    ]
    pads = pltpu.VMEM((2 * cols // LANES, PAD + rows, LANES), F32)
    key_work = (6 * rows * width * 2 * cols, 4 << 20)
    nrim, *other = call(
        first_key_kernel,
        [
            (sc, smem),
            *vmem(far_rim, near_rim, ew_own, ew_other, gain, normed),
            *vmem(wqkv[1], taps[1], feat_w[1]),
        ],
        [((RIM, width), BF16, None), *key_outs],
        "keys_other",
        [pads],
        key_work,
    )
    back = swap(other[3].astype(BF16), "rep", 1).astype(F32)
    own = call(
        key_kernel,
        [(sc, smem), *vmem(normed, nrim, wqkv[0], taps[0], feat_w[0]), (out_weight, hbm)],
        [*key_outs, (out_weight.shape, BF16, None)],
        "keys_own",
        [pads, pltpu.SemaphoreType.DMA],
        key_work,
    )
    ow = [own[6], swap(own[6], "rep", 1)]
    qf, local = [None] * 2, [None] * 2

    def query(k, keys, after):
        qf[k], local[k] = call(
            functools.partial(query_kernel, heads=heads),
            [(sc, smem), *vmem(after, normed, nrim, wqkv[k], taps[k], *keys[4:6], *keys[:2])],
            [((rows, feats), BF16, None), ((rows, 2 * cols), F32, None)],
            "queries",
            [pltpu.VMEM((cols // LANES, PAD + rows, LANES), F32)],
            (6 * rows * width * cols, 4 << 20),
        )

    covers = [functools.partial(query, 0, own), functools.partial(query, 1, other)]
    before = prefix(own[3] + back, "tm", masks, covers)
    state_own = before + jnp.where(second, back, 0.0)
    state_other = swap((before + jnp.where(second, 0.0, own[3])).astype(BF16), "rep", 1)

    (partial,) = call(
        functools.partial(own_kernel, heads=heads),
        vmem(qf[0], local[0], own[2], state_own, ow[0]),
        [((rows, width), F32, None)],
        "attend_own",
        (),
        (4 * rows * width * cols, 4 << 20),
    )
    return call(
        functools.partial(last_kernel, heads=heads),
        vmem(qf[1], local[1], other[2], state_other, ow[1], partial),
        [((rows, width), BF16, hbm)],
        "attend_other",
        [pltpu.VMEM((blocks, SUB, width), BF16), pltpu.SemaphoreType.DMA((blocks,))],
        (4 * rows * width * cols, 4 << 20),
    )[0]


def solution(mesh):
    in_specs = (
        P(("groups", "tm"), None),
        P("rep", None),
        P(),
        P(None, None, "rep"),
        P(None, None, "rep"),
        P("rep", None, None),
        P("rep", None),
    )
    out_specs = P(("groups", "tm", "rep"), None)
    return jax.shard_map(shards, mesh=mesh, in_specs=in_specs, out_specs=out_specs, check_vma=False)
```

```python
import functools
import math

import jax
import jax.numpy as jnp
from jax import lax
from jax.experimental import pallas as pl
from jax.experimental.pallas import tpu as pltpu
from jax.sharding import PartitionSpec as P

EPS = 1e-05
LOG2E = math.log2(math.e)
SUB = 256
STEP = 512
RIM = 16
PAD = 8
LANES = 128
F32 = jnp.float32
BF16 = jnp.bfloat16
NN = (((1,), (0,)), ((), ()))
NT = (((1,), (1,)), ((), ()))
TN = (((0,), (0,)), ((), ()))


def dot(a, b, dims=NN):
    return lax.dot_general(a, b, dims, preferred_element_type=F32)


def call(kernel, ins, outs, name, scratch=(), work=(1, 1), mib=16):
    def spec(place):
        return pl.BlockSpec(memory_space=pltpu.VMEM if place is None else place)

    def pinned(array, place):
        return pltpu.with_memory_space_constraint(array, place) if place is pltpu.HBM else array

    return pl.pallas_call(
        kernel,
        in_specs=[spec(p) for _, p in ins],
        out_specs=[spec(p) for _, _, p in outs],
        out_shape=[jax.ShapeDtypeStruct(s, t) for s, t, _ in outs],
        scratch_shapes=list(scratch),
        compiler_params=pltpu.CompilerParams(vmem_limit_bytes=mib << 20),
        cost_estimate=pl.CostEstimate(flops=work[0] << 3, bytes_accessed=work[1], transcendentals=0),
        name=name,
    )(*[pinned(*i) for i in ins])


def vmem(*arrays):
    return [(a, None) for a in arrays]


def normalize(emb, gain):
    mean = jnp.mean(emb * emb, -1, keepdims=True)
    return (emb * lax.rsqrt(mean + EPS) * gain).astype(BF16)


def rim_kernel(sc, sig, rim, sem):
    del sc
    copy = pltpu.make_async_copy(sig.at[pl.ds(sig.shape[0] - RIM, RIM), :], rim, sem)
    copy.start()
    copy.wait()


def embed_kernel(sc, sig, ew_a, ew_b, gain, normed, near_rim):
    rep = sc[0]
    rows = normed.shape[0]
    half = ew_a.shape[0]
    own = pl.ds(pl.multiple_of(rep * half, half), half)
    other = pl.ds(pl.multiple_of((1 - rep) * half, half), half)
    near_rim[...] = sig[rows - RIM : rows, :]
    for b in range(rows // STEP):
        at = pl.ds(pl.multiple_of(rep * rows + b * STEP, STEP), STEP)
        normed[b * STEP : (b + 1) * STEP, :] = normalize(
            dot(sig[at, own], ew_a[...]) + dot(sig[at, other], ew_b[...]), gain[...]
        )


def store_proj(pad, normed, weights, start):
    rows = normed.shape[0]
    c = 0
    for w in weights:
        proj = dot(normed, w).astype(BF16).astype(F32)
        for j in range(w.shape[1] // LANES):
            pad[c, start : start + rows, :] = proj[:, j * LANES : (j + 1) * LANES]
            c += 1


def convolve(pad, taps, part, first, count, start, rows):
    out = []
    for j in range(count):
        total = None
        for tap in range(taps.shape[1]):
            at = start - taps.shape[1] + 1 + tap
            weight = taps[part, tap : tap + 1, j * LANES : (j + 1) * LANES]
            term = weight * pad[first + j, at : at + rows, :]
            total = term if total is None else total + term
        out.append(total.astype(BF16))
    return jnp.concatenate(out, 1)


def features(part, diag, ones, heads):
    rows, width = part.shape[0], part.shape[1] // heads
    feat = diag.shape[1] // heads
    part_f = part.astype(F32)
    logits = dot(part, diag[...])
    squares = dot((part_f * part_f).astype(BF16), ones[...])
    scale = lax.rsqrt(squares * (1.0 / width) + EPS) * (LOG2E / math.sqrt(width))
    share = scale.shape[1] // heads
    out = []
    for h in range(heads):
        mine = jnp.broadcast_to(scale[:, h * share : h * share + 1], (rows, feat))
        out.append(jnp.exp2(logits[:, h * feat : (h + 1) * feat] * mine).astype(BF16))
    return jnp.concatenate(out, 1)


def rim_rows(pad, nrim, weights, keep):
    c = 0
    for w in weights:
        proj = dot(nrim, w).astype(BF16).astype(F32) * keep
        for j in range(w.shape[1] // LANES):
            pad[c, 0:PAD, :] = proj[RIM - PAD :, j * LANES : (j + 1) * LANES]
            c += 1


def key_body(sc, normed, nrim, weight, taps, feat_w, kf, val, before, total, diag, ones, pad):
    heads, head_dim, feat = feat_w.shape
    cols = val.shape[1]
    tiles = cols // LANES
    diag[...] = jnp.zeros_like(diag)
    share = LANES // heads
    of_row = lax.broadcasted_iota(jnp.int32, ones.shape, 0) // head_dim
    of_col = lax.broadcasted_iota(jnp.int32, ones.shape, 1) // share
    ones[...] = jnp.where(of_row == of_col, 1.0, 0.0).astype(BF16)
    for h in range(heads):
        diag[h * head_dim : (h + 1) * head_dim, h * feat : (h + 1) * feat] = feat_w[h]
    weights = (weight[1], weight[2])
    rim_rows(pad, nrim, weights, (sc[1] > 0).astype(F32))
    total[...] = jnp.zeros_like(total)
    rows = normed.shape[0]
    store_proj(pad, normed[...], weights, PAD)
    key = convolve(pad, taps, 1, 0, tiles, PAD, rows)
    value = convolve(pad, taps, 2, tiles, tiles, PAD, rows)
    val[...] = value
    key_feat = features(key, diag, ones, heads)
    kf[...] = key_feat
    for b in range(rows // SUB):
        sub = slice(b * SUB, (b + 1) * SUB)
        before[b] = total[...]
        for pair in range(heads // 2):
            vp = value[sub, pair * 2 * head_dim : (pair + 1) * 2 * head_dim]
            kp = key_feat[sub, pair * 2 * feat : (pair + 1) * 2 * feat]
            both = dot(vp, kp, TN)
            for side in range(2):
                h = pair * 2 + side
                total[h * head_dim : (h + 1) * head_dim, :] += both[
                    side * head_dim : (side + 1) * head_dim, side * feat : (side + 1) * feat
                ]
        sums = jnp.sum(key_feat[sub].astype(F32), 0, keepdims=True)
        for h in range(heads):
            at = heads * head_dim + h
            total[at : at + 1, :] += sums[:, h * feat : (h + 1) * feat]


def first_key_kernel(
    sc, far_rim, near_rim, ew_a, ew_b, gain, normed, weight, taps, feat_w,
    nrim, kf, val, before, total, diag, ones, pad,
):
    half = ew_a.shape[0]
    own = sc[0] == 0
    rim = jnp.where(own, far_rim[...].astype(F32), near_rim[...].astype(F32))
    lo, hi = rim[:, :half], rim[:, half:]
    mine = jnp.where(own, lo, hi).astype(BF16)
    other = jnp.where(own, hi, lo).astype(BF16)
    rows_n = normalize(dot(mine, ew_a[...]) + dot(other, ew_b[...]), gain[...])
    nrim[...] = rows_n
    key_body(sc, normed, rows_n, weight, taps, feat_w, kf, val, before, total, diag, ones, pad)


def key_kernel(
    sc, normed, nrim, weight, taps, feat_w, ow_hbm,
    kf, val, before, total, diag, ones, ow, pad, sem,
):
    copy = pltpu.make_async_copy(ow_hbm, ow, sem)
    copy.start()
    key_body(sc, normed, nrim[...], weight, taps, feat_w, kf, val, before, total, diag, ones, pad)
    copy.wait()


def query_kernel(
    sc, after, normed, nrim, weight, taps, diag, ones, kf, val, qf, out, pad, *, heads
):
    del after
    rows = normed.shape[0]
    feat = qf.shape[1] // heads
    width = val.shape[1] // heads
    row = lax.broadcasted_iota(jnp.int32, (SUB, SUB), 0)
    col = lax.broadcasted_iota(jnp.int32, (SUB, SUB), 1)
    causal = row >= col
    left = (lax.broadcasted_iota(jnp.int32, (SUB, 4 * width), 1) & (2 * width - 1)) < width
    one = jnp.ones((SUB, 2 * width), BF16)
    rim_rows(pad, nrim[...], (weight[0],), (sc[1] > 0).astype(F32))
    store_proj(pad, normed[...], (weight[0],), PAD)
    query = convolve(pad, taps, 0, 0, weight.shape[2] // LANES, PAD, rows)
    query_feat = features(query, diag, ones, heads)
    qf[...] = query_feat
    for b in range(rows // SUB):
        sub = slice(b * SUB, (b + 1) * SUB)
        for pair in range(heads // 2):
            weights = []
            for h in (2 * pair, 2 * pair + 1):
                at = slice(h * feat, (h + 1) * feat)
                scores = dot(query_feat[sub, at], kf[sub, at], NT)
                weights.append(jnp.where(causal, scores, 0.0).astype(BF16))
            vp = val[sub, pair * 2 * width : (pair + 1) * 2 * width]
            both = dot(jnp.concatenate(weights, 0), jnp.concatenate([vp, one], 1))
            out[sub, pair * 4 * width : (pair + 1) * 4 * width] = jnp.where(
                left, both[:SUB], both[SUB:]
            )


def attend(qf, local, before, state_in, b, heads):
    feat = qf.shape[1] // heads
    width = local.shape[1] // heads // 2
    zero = jnp.zeros((width, feat), BF16)
    rows = slice(b * SUB, (b + 1) * SUB)
    state = (before[b] + state_in).astype(BF16)
    out = []
    for pair in range(heads // 2):
        h = pair * 2
        s0, s1 = (state[(h + k) * width : (h + k + 1) * width] for k in range(2))
        t0, t1 = (
            jnp.broadcast_to(
                state[heads * width + h + k : heads * width + h + k + 1], (width, feat)
            )
            for k in range(2)
        )
        rhs = jnp.concatenate(
            [
                jnp.concatenate([s0, zero], 1),
                jnp.concatenate([zero, s1], 1),
                jnp.concatenate([t0, zero], 1),
                jnp.concatenate([zero, t1], 1),
            ],
            0,
        )
        both = local[rows, pair * 4 * width : (pair + 1) * 4 * width] + dot(
            qf[rows, pair * 2 * feat : (pair + 1) * 2 * feat], rhs, NT
        )
        out.append((both[:, : 2 * width] / both[:, 2 * width :]).astype(BF16))
    return jnp.concatenate(out, 1)


def own_kernel(qf, local, before, state, weight, out, *, heads):
    attended = [
        attend(qf, local, before, state[...], b, heads) for b in range(qf.shape[0] // SUB)
    ]
    out[...] = dot(jnp.concatenate(attended, 0), weight[...])


def last_kernel(qf, local, before, state, weight, partial, out, buf, sem, *, heads):
    copies = []
    state_in = state[...].astype(F32)
    per = buf.shape[1] // SUB
    for s in range(buf.shape[0]):
        attended = [
            attend(qf, local, before, state_in, s * per + b, heads) for b in range(per)
        ]
        rows = slice(s * per * SUB, (s + 1) * per * SUB)
        buf[s] = (partial[rows, :] + dot(jnp.concatenate(attended, 0), weight[...])).astype(BF16)
        copies.append(
            pltpu.make_async_copy(buf.at[s], out.at[pl.ds(s * per * SUB, per * SUB), :], sem.at[s])
        )
        copies[-1].start()
    for copy in copies:
        copy.wait()


def swap(array, axis, by):
    devices = lax.axis_size(axis)
    return lax.ppermute(array, axis, [(i, i ^ by) for i in range(devices)])


def rounds(axis):
    devices, span, out = lax.axis_size(axis), 1, []
    while span < devices:
        radix = min(4, devices // span)
        out.append((span, radix))
        span *= radix
    return out


def earlier(axis):
    place = lax.axis_index(axis)
    flags = []
    for span, radix in rounds(axis):
        digit = (place >> (span.bit_length() - 1)) & (radix - 1)
        flags += [(digit ^ k) < digit for k in range(1, radix)]
    return flags


def prefix(group, axis, masks, covers):
    near = jnp.zeros(group.shape, F32)
    row = 0
    for span, radix in rounds(axis):
        sent = group.astype(BF16)
        if covers:
            covers.pop(0)(sent)
        for k in range(1, radix):
            got = swap(sent, axis, k * span).astype(F32)
            group = group + got
            near = near + jnp.where(masks[row : row + 1] > 0, got, 0.0)
            row += 1
    while covers:
        covers.pop(0)(group)
    return near


def shards(signal, embed_weight, norm_gain, qkv_weight, conv_weight, feature_weight, out_weight):
    rows, depth = signal.shape
    rows //= 2
    half, width = embed_weight.shape
    cols = qkv_weight.shape[2]
    heads, head_dim, feat = feature_weight.shape
    feats = heads * feat
    states = heads * head_dim + 16
    blocks = rows // SUB
    place, rep = lax.axis_index("tm"), lax.axis_index("rep")
    devices = lax.axis_size("tm")
    smem, hbm = pltpu.SMEM, pltpu.HBM

    sc = jnp.stack([rep, 2 * place + rep]).astype(jnp.int32)
    flags = jnp.stack([rep > 0, *earlier("tm")]).astype(F32)
    masks = jnp.broadcast_to(flags[:, None], (flags.size, feat))
    sc, masks, signal, embed_weight, norm_gain, qkv_weight, conv_weight, feature_weight = (
        lax.optimization_barrier(
            (sc, masks, signal, embed_weight, norm_gain, qkv_weight, conv_weight, feature_weight)
        )
    )
    second, masks = masks[:1] > 0, masks[1:]
    ew_other = swap(embed_weight, "rep", 1)
    (far_rim,) = call(
        rim_kernel,
        [(sc, smem), (signal, hbm)],
        [((RIM, depth), BF16, None)],
        "rim",
        [pltpu.SemaphoreType.DMA],
        (1 << 30, 1 << 20),
    )
    far_rim = lax.ppermute(far_rim, "tm", [(i, (i + 1) % devices) for i in range(devices)])
    wqkv = [qkv_weight.transpose(1, 0, 2), swap(qkv_weight.transpose(1, 0, 2), "rep", 1)]
    taps = [conv_weight.transpose(1, 0, 2), swap(conv_weight.transpose(1, 0, 2), "rep", 1)]
    feat_w = [feature_weight, swap(feature_weight, "rep", 1)]
    gain = norm_gain.reshape(1, width)

    normed, near_rim = call(
        embed_kernel,
        [(sc, smem), *vmem(signal, embed_weight, ew_other, gain)],
        [((rows, width), BF16, None), ((RIM, depth), BF16, None)],
        "embed",
        (),
        (2 * rows * depth * width, 4 << 20),
    )

    key_outs = [
        ((rows, feats), BF16, None),
        ((rows, cols), BF16, None),
        ((blocks, states, feat), F32, None),
        ((states, feat), F32, None),
        ((cols, feats), BF16, None),
        ((cols, LANES), BF16, None),
    ]
    pads = pltpu.VMEM((2 * cols // LANES, PAD + rows, LANES), F32)
    key_work = (6 * rows * width * 2 * cols, 4 << 20)
    nrim, *other = call(
        first_key_kernel,
        [
            (sc, smem),
            *vmem(far_rim, near_rim, embed_weight, ew_other, gain, normed),
            *vmem(wqkv[1], taps[1], feat_w[1]),
        ],
        [((RIM, width), BF16, None), *key_outs],
        "keys_other",
        [pads],
        key_work,
    )
    back = swap(other[3].astype(BF16), "rep", 1).astype(F32)
    own = call(
        key_kernel,
        [(sc, smem), *vmem(normed, nrim, wqkv[0], taps[0], feat_w[0]), (out_weight, hbm)],
        [*key_outs, (out_weight.shape, BF16, None)],
        "keys_own",
        [pads, pltpu.SemaphoreType.DMA],
        key_work,
    )
    ow = [own[6], swap(own[6], "rep", 1)]
    qf, local = [None] * 2, [None] * 2

    def query(k, keys, after):
        qf[k], local[k] = call(
            functools.partial(query_kernel, heads=heads),
            [(sc, smem), *vmem(after, normed, nrim, wqkv[k], taps[k], *keys[4:6], *keys[:2])],
            [((rows, feats), BF16, None), ((rows, 2 * cols), F32, None)],
            "queries",
            [pltpu.VMEM((cols // LANES, PAD + rows, LANES), F32)],
            (6 * rows * width * cols, 4 << 20),
        )

    covers = [functools.partial(query, 0, own), functools.partial(query, 1, other)]
    before = prefix(own[3] + back, "tm", masks, covers)
    state_own = before + jnp.where(second, back, 0.0)
    state_other = swap((before + jnp.where(second, 0.0, own[3])).astype(BF16), "rep", 1)

    (partial,) = call(
        functools.partial(own_kernel, heads=heads),
        vmem(qf[0], local[0], own[2], state_own, ow[0]),
        [((rows, width), F32, None)],
        "attend_own",
        (),
        (4 * rows * width * cols, 4 << 20),
    )
    return call(
        functools.partial(last_kernel, heads=heads),
        vmem(qf[1], local[1], other[2], state_other, ow[1], partial),
        [((rows, width), BF16, hbm)],
        "attend_other",
        [pltpu.VMEM((2, rows // 2, width), BF16), pltpu.SemaphoreType.DMA((2,))],
        (4 * rows * width * cols, 4 << 20),
    )[0]


def solution(mesh):
    in_specs = (
        P(("groups", "tm"), None),
        P("rep", None),
        P(),
        P(None, None, "rep"),
        P(None, None, "rep"),
        P("rep", None, None),
        P("rep", None),
    )
    out_specs = P(("groups", "tm", "rep"), None)
    return jax.shard_map(shards, mesh=mesh, in_specs=in_specs, out_specs=out_specs, check_vma=False)
```

```python
import functools
import math

import jax
import jax.numpy as jnp
from jax import lax
from jax.experimental import pallas as pl
from jax.experimental.pallas import tpu as pltpu
from jax.sharding import PartitionSpec as P

EPS = 1e-05
LOG2E = math.log2(math.e)
SUB = 256
STEP = 512
RIM = 16
PAD = 8
LANES = 128
F32 = jnp.float32
BF16 = jnp.bfloat16
NN = (((1,), (0,)), ((), ()))
NT = (((1,), (1,)), ((), ()))
TN = (((0,), (0,)), ((), ()))


def dot(a, b, dims=NN):
    return lax.dot_general(a, b, dims, preferred_element_type=F32)


def call(kernel, ins, outs, name, scratch=(), work=(1, 1), mib=16):
    def spec(place):
        return pl.BlockSpec(memory_space=pltpu.VMEM if place is None else place)

    def pinned(array, place):
        return pltpu.with_memory_space_constraint(array, place) if place is pltpu.HBM else array

    return pl.pallas_call(
        kernel,
        in_specs=[spec(p) for _, p in ins],
        out_specs=[spec(p) for _, _, p in outs],
        out_shape=[jax.ShapeDtypeStruct(s, t) for s, t, _ in outs],
        scratch_shapes=list(scratch),
        compiler_params=pltpu.CompilerParams(vmem_limit_bytes=mib << 20),
        cost_estimate=pl.CostEstimate(flops=work[0] << 3, bytes_accessed=work[1], transcendentals=0),
        name=name,
    )(*[pinned(*i) for i in ins])


def vmem(*arrays):
    return [(a, None) for a in arrays]


def normalize(emb, gain):
    mean = jnp.mean(emb * emb, -1, keepdims=True)
    return (emb * lax.rsqrt(mean + EPS) * gain).astype(BF16)


def rim_kernel(after, sig, rim, sem):
    del after
    copy = pltpu.make_async_copy(sig.at[pl.ds(sig.shape[0] - RIM, RIM), :], rim, sem)
    copy.start()
    copy.wait()


def embed_kernel(sig, ew_a, ew_b, gain, normed, near_rim):
    rep = lax.axis_index("rep")
    rows = normed.shape[0]
    half = ew_a.shape[0]
    own = pl.ds(pl.multiple_of(rep * half, half), half)
    other = pl.ds(pl.multiple_of((1 - rep) * half, half), half)
    near_rim[...] = sig[rows - RIM : rows, :]
    for b in range(rows // STEP):
        at = pl.ds(pl.multiple_of(rep * rows + b * STEP, STEP), STEP)
        normed[b * STEP : (b + 1) * STEP, :] = normalize(
            dot(sig[at, own], ew_a[...]) + dot(sig[at, other], ew_b[...]), gain[...]
        )


def store_proj(pad, normed, weights, start):
    rows = normed.shape[0]
    c = 0
    for w in weights:
        proj = dot(normed, w).astype(BF16).astype(F32)
        for j in range(w.shape[1] // LANES):
            pad[c, start : start + rows, :] = proj[:, j * LANES : (j + 1) * LANES]
            c += 1


def convolve(pad, taps, part, first, count, start, rows):
    out = []
    for j in range(count):
        total = None
        for tap in range(taps.shape[1]):
            at = start - taps.shape[1] + 1 + tap
            weight = taps[part, tap : tap + 1, j * LANES : (j + 1) * LANES]
            term = weight * pad[first + j, at : at + rows, :]
            total = term if total is None else total + term
        out.append(total.astype(BF16))
    return jnp.concatenate(out, 1)


def features(part, diag, ones, heads):
    rows, width = part.shape[0], part.shape[1] // heads
    feat = diag.shape[1] // heads
    part_f = part.astype(F32)
    logits = dot(part, diag[...])
    squares = dot((part_f * part_f).astype(BF16), ones[...])
    scale = lax.rsqrt(squares * (1.0 / width) + EPS) * (LOG2E / math.sqrt(width))
    share = scale.shape[1] // heads
    out = []
    for h in range(heads):
        mine = jnp.broadcast_to(scale[:, h * share : h * share + 1], (rows, feat))
        out.append(jnp.exp2(logits[:, h * feat : (h + 1) * feat] * mine).astype(BF16))
    return jnp.concatenate(out, 1)


def rim_rows(pad, nrim, weights, masks):
    keep = masks[1:2, : weights[0].shape[1]]
    c = 0
    for w in weights:
        proj = dot(nrim, w).astype(BF16).astype(F32) * keep
        for j in range(w.shape[1] // LANES):
            pad[c, 0:PAD, :] = proj[RIM - PAD :, j * LANES : (j + 1) * LANES]
            c += 1


def key_body(masks, normed, nrim, weight, taps, feat_w, kf, val, before, total, diag, ones, pad):
    heads, head_dim, feat = feat_w.shape
    cols = val.shape[1]
    tiles = cols // LANES
    diag[...] = jnp.zeros_like(diag)
    share = LANES // heads
    of_row = lax.broadcasted_iota(jnp.int32, ones.shape, 0) // head_dim
    of_col = lax.broadcasted_iota(jnp.int32, ones.shape, 1) // share
    ones[...] = jnp.where(of_row == of_col, 1.0, 0.0).astype(BF16)
    for h in range(heads):
        diag[h * head_dim : (h + 1) * head_dim, h * feat : (h + 1) * feat] = feat_w[h]
    weights = (weight[1], weight[2])
    rim_rows(pad, nrim, weights, masks)
    total[...] = jnp.zeros_like(total)
    rows = normed.shape[0]
    store_proj(pad, normed[...], weights, PAD)
    key = convolve(pad, taps, 1, 0, tiles, PAD, rows)
    value = convolve(pad, taps, 2, tiles, tiles, PAD, rows)
    val[...] = value
    key_feat = features(key, diag, ones, heads)
    kf[...] = key_feat
    for b in range(rows // SUB):
        sub = slice(b * SUB, (b + 1) * SUB)
        before[b] = total[...]
        for pair in range(heads // 2):
            vp = value[sub, pair * 2 * head_dim : (pair + 1) * 2 * head_dim]
            kp = key_feat[sub, pair * 2 * feat : (pair + 1) * 2 * feat]
            both = dot(vp, kp, TN)
            for side in range(2):
                h = pair * 2 + side
                total[h * head_dim : (h + 1) * head_dim, :] += both[
                    side * head_dim : (side + 1) * head_dim, side * feat : (side + 1) * feat
                ]
        sums = jnp.sum(key_feat[sub].astype(F32), 0, keepdims=True)
        for h in range(heads):
            at = heads * head_dim + h
            total[at : at + 1, :] += sums[:, h * feat : (h + 1) * feat]


def first_key_kernel(
    masks, far_rim, near_rim, ew_a, ew_b, gain, normed, weight, taps, feat_w,
    nrim, kf, val, before, total, diag, ones, pad,
):
    half = ew_a.shape[0]
    own = jnp.broadcast_to(masks[0:1, :], (RIM, half)) == 0
    far, near = far_rim[...].astype(F32), near_rim[...].astype(F32)
    rim = jnp.concatenate(
        [jnp.where(own, far[:, :half], near[:, :half]), jnp.where(own, far[:, half:], near[:, half:])],
        1,
    )
    lo, hi = rim[:, :half], rim[:, half:]
    mine = jnp.where(own, lo, hi).astype(BF16)
    other = jnp.where(own, hi, lo).astype(BF16)
    rows_n = normalize(dot(mine, ew_a[...]) + dot(other, ew_b[...]), gain[...])
    nrim[...] = rows_n
    key_body(masks, normed, rows_n, weight, taps, feat_w, kf, val, before, total, diag, ones, pad)


def key_kernel(
    masks, normed, nrim, weight, taps, feat_w, ow_hbm,
    kf, val, before, total, diag, ones, ow, pad, sem,
):
    copy = pltpu.make_async_copy(ow_hbm, ow, sem)
    copy.start()
    key_body(masks, normed, nrim[...], weight, taps, feat_w, kf, val, before, total, diag, ones, pad)
    copy.wait()


def query_kernel(
    masks, after, normed, nrim, weight, taps, diag, ones, kf, val, qf, out, pad, *, heads
):
    del after
    rows = normed.shape[0]
    feat = qf.shape[1] // heads
    width = val.shape[1] // heads
    row = lax.broadcasted_iota(jnp.int32, (SUB, SUB), 0)
    col = lax.broadcasted_iota(jnp.int32, (SUB, SUB), 1)
    causal = row >= col
    left = (lax.broadcasted_iota(jnp.int32, (SUB, 4 * width), 1) & (2 * width - 1)) < width
    one = jnp.ones((SUB, 2 * width), BF16)
    rim_rows(pad, nrim[...], (weight[0],), masks)
    store_proj(pad, normed[...], (weight[0],), PAD)
    query = convolve(pad, taps, 0, 0, weight.shape[2] // LANES, PAD, rows)
    query_feat = features(query, diag, ones, heads)
    qf[...] = query_feat
    for b in range(rows // SUB):
        sub = slice(b * SUB, (b + 1) * SUB)
        for pair in range(heads // 2):
            weights = []
            for h in (2 * pair, 2 * pair + 1):
                at = slice(h * feat, (h + 1) * feat)
                scores = dot(query_feat[sub, at], kf[sub, at], NT)
                weights.append(jnp.where(causal, scores, 0.0).astype(BF16))
            vp = val[sub, pair * 2 * width : (pair + 1) * 2 * width]
            both = dot(jnp.concatenate(weights, 0), jnp.concatenate([vp, one], 1))
            out[sub, pair * 4 * width : (pair + 1) * 4 * width] = jnp.where(
                left, both[:SUB], both[SUB:]
            )


def attend(qf, local, before, state_in, b, heads):
    feat = qf.shape[1] // heads
    width = local.shape[1] // heads // 2
    zero = jnp.zeros((width, feat), BF16)
    rows = slice(b * SUB, (b + 1) * SUB)
    state = (before[b] + state_in).astype(BF16)
    out = []
    for pair in range(heads // 2):
        h = pair * 2
        s0, s1 = (state[(h + k) * width : (h + k + 1) * width] for k in range(2))
        t0, t1 = (
            jnp.broadcast_to(
                state[heads * width + h + k : heads * width + h + k + 1], (width, feat)
            )
            for k in range(2)
        )
        rhs = jnp.concatenate(
            [
                jnp.concatenate([s0, zero], 1),
                jnp.concatenate([zero, s1], 1),
                jnp.concatenate([t0, zero], 1),
                jnp.concatenate([zero, t1], 1),
            ],
            0,
        )
        both = local[rows, pair * 4 * width : (pair + 1) * 4 * width] + dot(
            qf[rows, pair * 2 * feat : (pair + 1) * 2 * feat], rhs, NT
        )
        out.append((both[:, : 2 * width] / both[:, 2 * width :]).astype(BF16))
    return jnp.concatenate(out, 1)


def own_kernel(qf, local, before, state, weight, out, *, heads):
    attended = [
        attend(qf, local, before, state[...], b, heads) for b in range(qf.shape[0] // SUB)
    ]
    out[...] = dot(jnp.concatenate(attended, 0), weight[...])


def last_kernel(qf, local, before, state, weight, partial, out, buf, sem, *, heads):
    copies = []
    state_in = state[...].astype(F32)
    per = buf.shape[1] // SUB
    for s in range(buf.shape[0]):
        attended = [
            attend(qf, local, before, state_in, s * per + b, heads) for b in range(per)
        ]
        rows = slice(s * per * SUB, (s + 1) * per * SUB)
        buf[s] = (partial[rows, :] + dot(jnp.concatenate(attended, 0), weight[...])).astype(BF16)
        copies.append(
            pltpu.make_async_copy(buf.at[s], out.at[pl.ds(s * per * SUB, per * SUB), :], sem.at[s])
        )
        copies[-1].start()
    for copy in copies:
        copy.wait()


def swap(array, axis, by):
    devices = lax.axis_size(axis)
    return lax.ppermute(array, axis, [(i, i ^ by) for i in range(devices)])


def rounds(axis):
    devices, span, out = lax.axis_size(axis), 1, []
    while span < devices:
        radix = min(4, devices // span)
        out.append((span, radix))
        span *= radix
    return out


def earlier(axis):
    place = lax.axis_index(axis)
    flags = []
    for span, radix in rounds(axis):
        digit = (place >> (span.bit_length() - 1)) & (radix - 1)
        flags += [(digit ^ k) < digit for k in range(1, radix)]
    return flags


def prefix(group, axis, masks, covers):
    near = jnp.zeros(group.shape, F32)
    row = 0
    for span, radix in rounds(axis):
        sent = group.astype(BF16)
        if covers:
            covers.pop(0)(sent)
        for k in range(1, radix):
            got = swap(sent, axis, k * span).astype(F32)
            group = group + got
            near = near + jnp.where(masks[row : row + 1] > 0, got, 0.0)
            row += 1
    while covers:
        covers.pop(0)(group)
    return near


def shards(signal, embed_weight, norm_gain, qkv_weight, conv_weight, feature_weight, out_weight):
    rows, depth = signal.shape
    rows //= 2
    half, width = embed_weight.shape
    cols = qkv_weight.shape[2]
    heads, head_dim, feat = feature_weight.shape
    feats = heads * feat
    states = heads * head_dim + 16
    blocks = rows // SUB
    place, rep = lax.axis_index("tm"), lax.axis_index("rep")
    devices = lax.axis_size("tm")
    hbm = pltpu.HBM

    flags = jnp.stack([rep > 0, 2 * place + rep > 0, *earlier("tm")]).astype(F32)
    masks = jnp.broadcast_to(flags[:, None], (flags.size, half))
    masks, signal, embed_weight, norm_gain, qkv_weight, conv_weight, feature_weight = (
        lax.optimization_barrier(
            (masks, signal, embed_weight, norm_gain, qkv_weight, conv_weight, feature_weight)
        )
    )
    second = masks[:1, :feat] > 0
    ew_other = swap(embed_weight, "rep", 1)
    (far_rim,) = call(
        rim_kernel,
        [(masks, None), (signal, hbm)],
        [((RIM, depth), BF16, None)],
        "rim",
        [pltpu.SemaphoreType.DMA],
        (1 << 30, 1 << 20),
    )
    far_rim = lax.ppermute(far_rim, "tm", [(i, (i + 1) % devices) for i in range(devices)])
    wqkv = [qkv_weight.transpose(1, 0, 2), swap(qkv_weight.transpose(1, 0, 2), "rep", 1)]
    taps = [conv_weight.transpose(1, 0, 2), swap(conv_weight.transpose(1, 0, 2), "rep", 1)]
    feat_w = [feature_weight, swap(feature_weight, "rep", 1)]
    gain = norm_gain.reshape(1, width)

    normed, near_rim = call(
        embed_kernel,
        vmem(signal, embed_weight, ew_other, gain),
        [((rows, width), BF16, None), ((RIM, depth), BF16, None)],
        "embed",
        (),
        (2 * rows * depth * width, 4 << 20),
    )

    key_outs = [
        ((rows, feats), BF16, None),
        ((rows, cols), BF16, None),
        ((blocks, states, feat), F32, None),
        ((states, feat), F32, None),
        ((cols, feats), BF16, None),
        ((cols, LANES), BF16, None),
    ]
    pads = pltpu.VMEM((2 * cols // LANES, PAD + rows, LANES), F32)
    key_work = (6 * rows * width * 2 * cols, 4 << 20)
    nrim, *other = call(
        first_key_kernel,
        [
            *vmem(masks, far_rim, near_rim, embed_weight, ew_other, gain, normed),
            *vmem(wqkv[1], taps[1], feat_w[1]),
        ],
        [((RIM, width), BF16, None), *key_outs],
        "keys_other",
        [pads],
        key_work,
    )
    back = swap(other[3].astype(BF16), "rep", 1).astype(F32)
    own = call(
        key_kernel,
        [*vmem(masks, normed, nrim, wqkv[0], taps[0], feat_w[0]), (out_weight, hbm)],
        [*key_outs, (out_weight.shape, BF16, None)],
        "keys_own",
        [pads, pltpu.SemaphoreType.DMA],
        key_work,
    )
    ow = [own[6], swap(own[6], "rep", 1)]
    qf, local = [None] * 2, [None] * 2

    def query(k, keys, after):
        qf[k], local[k] = call(
            functools.partial(query_kernel, heads=heads),
            [*vmem(masks, after, normed, nrim, wqkv[k], taps[k], *keys[4:6], *keys[:2])],
            [((rows, feats), BF16, None), ((rows, 2 * cols), F32, None)],
            "queries",
            [pltpu.VMEM((cols // LANES, PAD + rows, LANES), F32)],
            (6 * rows * width * cols, 4 << 20),
        )

    covers = [functools.partial(query, 0, own), functools.partial(query, 1, other)]
    before = prefix(own[3] + back, "tm", masks[2:, :feat], covers)
    state_own = before + jnp.where(second, back, 0.0)
    state_other = swap((before + jnp.where(second, 0.0, own[3])).astype(BF16), "rep", 1)

    (partial,) = call(
        functools.partial(own_kernel, heads=heads),
        vmem(qf[0], local[0], own[2], state_own, ow[0]),
        [((rows, width), F32, None)],
        "attend_own",
        (),
        (4 * rows * width * cols, 4 << 20),
    )
    return call(
        functools.partial(last_kernel, heads=heads),
        vmem(qf[1], local[1], other[2], state_other, ow[1], partial),
        [((rows, width), BF16, hbm)],
        "attend_other",
        [pltpu.VMEM((2, rows // 2, width), BF16), pltpu.SemaphoreType.DMA((2,))],
        (4 * rows * width * cols, 4 << 20),
    )[0]


def solution(mesh):
    in_specs = (
        P(("groups", "tm"), None),
        P("rep", None),
        P(),
        P(None, None, "rep"),
        P(None, None, "rep"),
        P("rep", None, None),
        P("rep", None),
    )
    out_specs = P(("groups", "tm", "rep"), None)
    return jax.shard_map(shards, mesh=mesh, in_specs=in_specs, out_specs=out_specs, check_vma=False)
```

```python
import functools
import math

import jax
import jax.numpy as jnp
from jax import lax
from jax.experimental import pallas as pl
from jax.experimental.pallas import tpu as pltpu
from jax.sharding import PartitionSpec as P

EPS = 1e-05
LOG2E = math.log2(math.e)
SUB = 256
STEP = 512
RIM = 16
PAD = 8
LANES = 128
F32 = jnp.float32
BF16 = jnp.bfloat16
NN = (((1,), (0,)), ((), ()))
NT = (((1,), (1,)), ((), ()))
TN = (((0,), (0,)), ((), ()))


def dot(a, b, dims=NN):
    return lax.dot_general(a, b, dims, preferred_element_type=F32)


def call(kernel, ins, outs, name, scratch=(), work=(1, 1), mib=16):
    def spec(place):
        return pl.BlockSpec(memory_space=pltpu.VMEM if place is None else place)

    def pinned(array, place):
        return pltpu.with_memory_space_constraint(array, place) if place is pltpu.HBM else array

    return pl.pallas_call(
        kernel,
        in_specs=[spec(p) for _, p in ins],
        out_specs=[spec(p) for _, _, p in outs],
        out_shape=[jax.ShapeDtypeStruct(s, t) for s, t, _ in outs],
        scratch_shapes=list(scratch),
        compiler_params=pltpu.CompilerParams(vmem_limit_bytes=mib << 20),
        cost_estimate=pl.CostEstimate(flops=work[0] << 3, bytes_accessed=work[1], transcendentals=0),
        name=name,
    )(*[pinned(*i) for i in ins])


def vmem(*arrays):
    return [(a, None) for a in arrays]


def normalize(emb, gain):
    mean = jnp.mean(emb * emb, -1, keepdims=True)
    return (emb * lax.rsqrt(mean + EPS) * gain).astype(BF16)


def rim_kernel(after, sig, rim, sem):
    del after
    copy = pltpu.make_async_copy(sig.at[pl.ds(sig.shape[0] - RIM, RIM), :], rim, sem)
    copy.start()
    copy.wait()


def embed_kernel(sig, ew_a, ew_b, gain, normed, near_rim):
    rep = lax.axis_index("rep")
    rows = normed.shape[0]
    half = ew_a.shape[0]
    own = pl.ds(pl.multiple_of(rep * half, half), half)
    other = pl.ds(pl.multiple_of((1 - rep) * half, half), half)
    near_rim[...] = sig[rows - RIM : rows, :]
    for b in range(rows // STEP):
        at = pl.ds(pl.multiple_of(rep * rows + b * STEP, STEP), STEP)
        normed[b * STEP : (b + 1) * STEP, :] = normalize(
            dot(sig[at, own], ew_a[...]) + dot(sig[at, other], ew_b[...]), gain[...]
        )


def store_proj(pad, normed, weights, start):
    rows = normed.shape[0]
    c = 0
    for w in weights:
        proj = dot(normed, w).astype(BF16).astype(F32)
        for j in range(w.shape[1] // LANES):
            pad[c, start : start + rows, :] = proj[:, j * LANES : (j + 1) * LANES]
            c += 1


def convolve(pad, taps, part, first, count, start, rows):
    out = []
    for j in range(count):
        total = None
        for tap in range(taps.shape[1]):
            at = start - taps.shape[1] + 1 + tap
            weight = taps[part, tap : tap + 1, j * LANES : (j + 1) * LANES]
            term = weight * pad[first + j, at : at + rows, :]
            total = term if total is None else total + term
        out.append(total.astype(BF16))
    return jnp.concatenate(out, 1)


def features(part, diag, ones, heads, together):
    rows, width = part.shape[0], part.shape[1] // heads
    feat, share = diag.shape[1] // heads, ones.shape[1] // heads
    part_f = part.astype(F32)
    out = []
    for first in range(0, heads, together):
        at = slice(first * width, (first + together) * width)
        logits = dot(part[:, at], diag[at, first * feat : (first + together) * feat])
        squares = dot((part_f[:, at] * part_f[:, at]).astype(BF16), ones[at, :])
        scale = lax.rsqrt(squares * (1.0 / width) + EPS) * (LOG2E / math.sqrt(width))
        for k in range(together):
            lane = (first + k) * share
            mine = jnp.broadcast_to(scale[:, lane : lane + 1], (rows, feat))
            out.append(jnp.exp2(logits[:, k * feat : (k + 1) * feat] * mine).astype(BF16))
    return jnp.concatenate(out, 1)


def rim_rows(pad, nrim, weights, masks):
    keep = masks[1:2, : weights[0].shape[1]]
    c = 0
    for w in weights:
        proj = dot(nrim, w).astype(BF16).astype(F32) * keep
        for j in range(w.shape[1] // LANES):
            pad[c, 0:PAD, :] = proj[RIM - PAD :, j * LANES : (j + 1) * LANES]
            c += 1


def key_body(masks, normed, nrim, weight, taps, feat_w, kf, val, before, total, diag, ones, pad):
    heads, head_dim, feat = feat_w.shape
    cols = val.shape[1]
    tiles = cols // LANES
    diag[...] = jnp.zeros_like(diag)
    share = LANES // heads
    of_row = lax.broadcasted_iota(jnp.int32, ones.shape, 0) // head_dim
    of_col = lax.broadcasted_iota(jnp.int32, ones.shape, 1) // share
    ones[...] = jnp.where(of_row == of_col, 1.0, 0.0).astype(BF16)
    for h in range(heads):
        diag[h * head_dim : (h + 1) * head_dim, h * feat : (h + 1) * feat] = feat_w[h]
    weights = (weight[1], weight[2])
    rim_rows(pad, nrim, weights, masks)
    total[...] = jnp.zeros_like(total)
    rows = normed.shape[0]
    store_proj(pad, normed[...], weights, PAD)
    key = convolve(pad, taps, 1, 0, tiles, PAD, rows)
    value = convolve(pad, taps, 2, tiles, tiles, PAD, rows)
    val[...] = value
    key_feat = features(key, diag, ones, heads, 2)
    kf[...] = key_feat
    for b in range(rows // SUB):
        sub = slice(b * SUB, (b + 1) * SUB)
        before[b] = total[...]
        for pair in range(heads // 2):
            vp = value[sub, pair * 2 * head_dim : (pair + 1) * 2 * head_dim]
            kp = key_feat[sub, pair * 2 * feat : (pair + 1) * 2 * feat]
            both = dot(vp, kp, TN)
            for side in range(2):
                h = pair * 2 + side
                total[h * head_dim : (h + 1) * head_dim, :] += both[
                    side * head_dim : (side + 1) * head_dim, side * feat : (side + 1) * feat
                ]
        sums = jnp.sum(key_feat[sub].astype(F32), 0, keepdims=True)
        for h in range(heads):
            at = heads * head_dim + h
            total[at : at + 1, :] += sums[:, h * feat : (h + 1) * feat]


def first_key_kernel(
    masks, far_rim, near_rim, ew_a, ew_b, gain, normed, weight, taps, feat_w,
    nrim, kf, val, before, total, diag, ones, pad,
):
    half = ew_a.shape[0]
    own = jnp.broadcast_to(masks[0:1, :], (RIM, half)) == 0
    far, near = far_rim[...].astype(F32), near_rim[...].astype(F32)
    rim = jnp.concatenate(
        [jnp.where(own, far[:, :half], near[:, :half]), jnp.where(own, far[:, half:], near[:, half:])],
        1,
    )
    lo, hi = rim[:, :half], rim[:, half:]
    mine = jnp.where(own, lo, hi).astype(BF16)
    other = jnp.where(own, hi, lo).astype(BF16)
    rows_n = normalize(dot(mine, ew_a[...]) + dot(other, ew_b[...]), gain[...])
    nrim[...] = rows_n
    key_body(masks, normed, rows_n, weight, taps, feat_w, kf, val, before, total, diag, ones, pad)


def key_kernel(
    masks, normed, nrim, weight, taps, feat_w, ow_hbm,
    kf, val, before, total, diag, ones, ow, pad, sem,
):
    copy = pltpu.make_async_copy(ow_hbm, ow, sem)
    copy.start()
    key_body(masks, normed, nrim[...], weight, taps, feat_w, kf, val, before, total, diag, ones, pad)
    copy.wait()


def query_kernel(
    masks, after, normed, nrim, weight, taps, diag, ones, kf, val, qf, out, pad, *, heads
):
    del after
    rows = normed.shape[0]
    feat = qf.shape[1] // heads
    width = val.shape[1] // heads
    row = lax.broadcasted_iota(jnp.int32, (SUB, SUB), 0)
    col = lax.broadcasted_iota(jnp.int32, (SUB, SUB), 1)
    causal = row >= col
    left = (lax.broadcasted_iota(jnp.int32, (SUB, 4 * width), 1) & (2 * width - 1)) < width
    one = jnp.ones((SUB, 2 * width), BF16)
    rim_rows(pad, nrim[...], (weight[0],), masks)
    store_proj(pad, normed[...], (weight[0],), PAD)
    query = convolve(pad, taps, 0, 0, weight.shape[2] // LANES, PAD, rows)
    query_feat = features(query, diag, ones, heads, heads)
    qf[...] = query_feat
    for b in range(rows // SUB):
        sub = slice(b * SUB, (b + 1) * SUB)
        for pair in range(heads // 2):
            weights = []
            for h in (2 * pair, 2 * pair + 1):
                at = slice(h * feat, (h + 1) * feat)
                scores = dot(query_feat[sub, at], kf[sub, at], NT)
                weights.append(jnp.where(causal, scores, 0.0).astype(BF16))
            vp = val[sub, pair * 2 * width : (pair + 1) * 2 * width]
            both = dot(jnp.concatenate(weights, 0), jnp.concatenate([vp, one], 1))
            out[sub, pair * 4 * width : (pair + 1) * 4 * width] = jnp.where(
                left, both[:SUB], both[SUB:]
            )


def attend(qf, local, before, state_in, b, heads):
    feat = qf.shape[1] // heads
    width = local.shape[1] // heads // 2
    zero = jnp.zeros((width, feat), BF16)
    rows = slice(b * SUB, (b + 1) * SUB)
    state = (before[b] + state_in).astype(BF16)
    out = []
    for pair in range(heads // 2):
        h = pair * 2
        s0, s1 = (state[(h + k) * width : (h + k + 1) * width] for k in range(2))
        t0, t1 = (
            jnp.broadcast_to(
                state[heads * width + h + k : heads * width + h + k + 1], (width, feat)
            )
            for k in range(2)
        )
        rhs = jnp.concatenate(
            [
                jnp.concatenate([s0, zero], 1),
                jnp.concatenate([zero, s1], 1),
                jnp.concatenate([t0, zero], 1),
                jnp.concatenate([zero, t1], 1),
            ],
            0,
        )
        both = local[rows, pair * 4 * width : (pair + 1) * 4 * width] + dot(
            qf[rows, pair * 2 * feat : (pair + 1) * 2 * feat], rhs, NT
        )
        out.append((both[:, : 2 * width] / both[:, 2 * width :]).astype(BF16))
    return jnp.concatenate(out, 1)


def own_kernel(qf, local, before, state, weight, out, *, heads):
    attended = [
        attend(qf, local, before, state[...], b, heads) for b in range(qf.shape[0] // SUB)
    ]
    out[...] = dot(jnp.concatenate(attended, 0), weight[...])


def last_kernel(qf, local, before, state, weight, partial, out, buf, sem, *, heads):
    copies = []
    state_in = state[...].astype(F32)
    per = buf.shape[1] // SUB
    for s in range(buf.shape[0]):
        attended = [
            attend(qf, local, before, state_in, s * per + b, heads) for b in range(per)
        ]
        rows = slice(s * per * SUB, (s + 1) * per * SUB)
        buf[s] = (partial[rows, :] + dot(jnp.concatenate(attended, 0), weight[...])).astype(BF16)
        copies.append(
            pltpu.make_async_copy(buf.at[s], out.at[pl.ds(s * per * SUB, per * SUB), :], sem.at[s])
        )
        copies[-1].start()
    for copy in copies:
        copy.wait()


def swap(array, axis, by):
    devices = lax.axis_size(axis)
    return lax.ppermute(array, axis, [(i, i ^ by) for i in range(devices)])


def rounds(axis):
    devices, span, out = lax.axis_size(axis), 1, []
    while span < devices:
        radix = min(4, devices // span)
        out.append((span, radix))
        span *= radix
    return out


def earlier(axis):
    place = lax.axis_index(axis)
    flags = []
    for span, radix in rounds(axis):
        digit = (place >> (span.bit_length() - 1)) & (radix - 1)
        flags += [(digit ^ k) < digit for k in range(1, radix)]
    return flags


def prefix(group, axis, masks, covers):
    near = jnp.zeros(group.shape, F32)
    row = 0
    for span, radix in rounds(axis):
        sent = group.astype(BF16)
        if covers:
            covers.pop(0)(sent)
        for k in range(1, radix):
            got = swap(sent, axis, k * span).astype(F32)
            group = group + got
            near = near + jnp.where(masks[row : row + 1] > 0, got, 0.0)
            row += 1
    while covers:
        covers.pop(0)(group)
    return near


def shards(signal, embed_weight, norm_gain, qkv_weight, conv_weight, feature_weight, out_weight):
    rows, depth = signal.shape
    rows //= 2
    half, width = embed_weight.shape
    cols = qkv_weight.shape[2]
    heads, head_dim, feat = feature_weight.shape
    feats = heads * feat
    states = heads * head_dim + 16
    blocks = rows // SUB
    place, rep = lax.axis_index("tm"), lax.axis_index("rep")
    devices = lax.axis_size("tm")
    hbm = pltpu.HBM

    flags = jnp.stack([rep > 0, 2 * place + rep > 0, *earlier("tm")]).astype(F32)
    masks = jnp.broadcast_to(flags[:, None], (flags.size, half))
    masks, signal, embed_weight, norm_gain, qkv_weight, conv_weight, feature_weight = (
        lax.optimization_barrier(
            (masks, signal, embed_weight, norm_gain, qkv_weight, conv_weight, feature_weight)
        )
    )
    second = masks[:1, :feat] > 0
    ew_other = swap(embed_weight, "rep", 1)
    (far_rim,) = call(
        rim_kernel,
        [(masks, None), (signal, hbm)],
        [((RIM, depth), BF16, None)],
        "rim",
        [pltpu.SemaphoreType.DMA],
        (1 << 30, 1 << 20),
    )
    ring = [(2 * i, 2 * i + 2) for i in range(devices - 1)] + [(2 * devices - 2, 2 * devices - 1)]
    ring += [(2 * i + 1, 2 * i - 1) for i in range(1, devices)] + [(1, 0)]
    far_rim = lax.ppermute(far_rim, ("tm", "rep"), ring)
    wqkv = [qkv_weight.transpose(1, 0, 2), swap(qkv_weight.transpose(1, 0, 2), "rep", 1)]
    taps = [conv_weight.transpose(1, 0, 2), swap(conv_weight.transpose(1, 0, 2), "rep", 1)]
    feat_w = [feature_weight, swap(feature_weight, "rep", 1)]
    gain = norm_gain.reshape(1, width)

    normed, near_rim = call(
        embed_kernel,
        vmem(signal, embed_weight, ew_other, gain),
        [((rows, width), BF16, None), ((RIM, depth), BF16, None)],
        "embed",
        (),
        (2 * rows * depth * width, 4 << 20),
    )

    key_outs = [
        ((rows, feats), BF16, None),
        ((rows, cols), BF16, None),
        ((blocks, states, feat), F32, None),
        ((states, feat), F32, None),
        ((cols, feats), BF16, None),
        ((cols, LANES), BF16, None),
    ]
    pads = pltpu.VMEM((2 * cols // LANES, PAD + rows, LANES), F32)
    key_work = (6 * rows * width * 2 * cols, 4 << 20)
    nrim, *other = call(
        first_key_kernel,
        [
            *vmem(masks, far_rim, near_rim, embed_weight, ew_other, gain, normed),
            *vmem(wqkv[1], taps[1], feat_w[1]),
        ],
        [((RIM, width), BF16, None), *key_outs],
        "keys_other",
        [pads],
        key_work,
    )
    back = swap(other[3].astype(BF16), "rep", 1).astype(F32)
    own = call(
        key_kernel,
        [*vmem(masks, normed, nrim, wqkv[0], taps[0], feat_w[0]), (out_weight, hbm)],
        [*key_outs, (out_weight.shape, BF16, None)],
        "keys_own",
        [pads, pltpu.SemaphoreType.DMA],
        key_work,
    )
    qf, local, ow = [None] * 2, [None] * 2, [own[6]]

    def query(k, keys, after):
        qf[k], local[k] = call(
            functools.partial(query_kernel, heads=heads),
            vmem(masks, after, normed, nrim, wqkv[k], taps[k], *keys[4:6], *keys[:2]),
            [((rows, feats), BF16, None), ((rows, 2 * cols), F32, None)],
            "queries",
            [pltpu.VMEM((cols // LANES, PAD + rows, LANES), F32)],
            (6 * rows * width * cols, 4 << 20),
        )
        if k == 1:
            ow.append(swap(lax.optimization_barrier((ow[0], after))[0], "rep", 1))

    covers = [functools.partial(query, 0, own), functools.partial(query, 1, other)]
    before = prefix(own[3] + back, "tm", masks[2:, :feat], covers)
    state_own = before + jnp.where(second, back, 0.0)
    state_other = swap((before + jnp.where(second, 0.0, own[3])).astype(BF16), "rep", 1)

    (partial,) = call(
        functools.partial(own_kernel, heads=heads),
        vmem(qf[0], local[0], own[2], state_own, ow[0]),
        [((rows, width), F32, None)],
        "attend_own",
        (),
        (4 * rows * width * cols, 4 << 20),
    )
    return call(
        functools.partial(last_kernel, heads=heads),
        vmem(qf[1], local[1], other[2], state_other, ow[1], partial),
        [((rows, width), BF16, hbm)],
        "attend_other",
        [pltpu.VMEM((2, rows // 2, width), BF16), pltpu.SemaphoreType.DMA((2,))],
        (4 * rows * width * cols, 4 << 20),
    )[0]


def solution(mesh):
    in_specs = (
        P(("groups", "tm"), None),
        P("rep", None),
        P(),
        P(None, None, "rep"),
        P(None, None, "rep"),
        P("rep", None, None),
        P("rep", None),
    )
    out_specs = P(("groups", "tm", "rep"), None)
    return jax.shard_map(shards, mesh=mesh, in_specs=in_specs, out_specs=out_specs, check_vma=False)
```

```python
import functools
import math

import jax
import jax.numpy as jnp
from jax import lax
from jax.experimental import pallas as pl
from jax.experimental.pallas import tpu as pltpu
from jax.sharding import PartitionSpec as P

EPS = 1e-05
LOG2E = math.log2(math.e)
SUB = 256
STEP = 512
RIM = 16
PAD = 8
LANES = 128
F32 = jnp.float32
BF16 = jnp.bfloat16
NN = (((1,), (0,)), ((), ()))
NT = (((1,), (1,)), ((), ()))
TN = (((0,), (0,)), ((), ()))


def dot(a, b, dims=NN):
    return lax.dot_general(a, b, dims, preferred_element_type=F32)


def call(kernel, ins, outs, name, scratch=(), work=(1, 1), mib=16):
    def spec(place):
        return pl.BlockSpec(memory_space=pltpu.VMEM if place is None else place)

    def pinned(array, place):
        return pltpu.with_memory_space_constraint(array, place) if place is pltpu.HBM else array

    return pl.pallas_call(
        kernel,
        in_specs=[spec(p) for _, p in ins],
        out_specs=[spec(p) for _, _, p in outs],
        out_shape=[jax.ShapeDtypeStruct(s, t) for s, t, _ in outs],
        scratch_shapes=list(scratch),
        compiler_params=pltpu.CompilerParams(vmem_limit_bytes=mib << 20),
        cost_estimate=pl.CostEstimate(flops=work[0] << 3, bytes_accessed=work[1], transcendentals=0),
        name=name,
    )(*[pinned(*i) for i in ins])


def vmem(*arrays):
    return [(a, None) for a in arrays]


def normalize(emb, gain):
    mean = jnp.mean(emb * emb, -1, keepdims=True)
    return (emb * lax.rsqrt(mean + EPS) * gain).astype(BF16)


def rim_kernel(after, sig, rim, sem):
    del after
    copy = pltpu.make_async_copy(sig.at[pl.ds(sig.shape[0] - RIM, RIM), :], rim, sem)
    copy.start()
    copy.wait()


def embed_kernel(sig, ew_a, ew_b, gain, normed, near_rim):
    rep = lax.axis_index("rep")
    rows = normed.shape[0]
    half = ew_a.shape[0]
    own = pl.ds(pl.multiple_of(rep * half, half), half)
    other = pl.ds(pl.multiple_of((1 - rep) * half, half), half)
    near_rim[...] = sig[rows - RIM : rows, :]
    for b in range(rows // STEP):
        at = pl.ds(pl.multiple_of(rep * rows + b * STEP, STEP), STEP)
        normed[b * STEP : (b + 1) * STEP, :] = normalize(
            dot(sig[at, own], ew_a[...]) + dot(sig[at, other], ew_b[...]), gain[...]
        )


def store_proj(pad, normed, weights, start):
    rows = normed.shape[0]
    c = 0
    for w in weights:
        proj = dot(normed, w).astype(BF16).astype(F32)
        for j in range(w.shape[1] // LANES):
            pad[c, start : start + rows, :] = proj[:, j * LANES : (j + 1) * LANES]
            c += 1


def convolve(pad, taps, part, first, count, start, rows):
    out = []
    for j in range(count):
        total = None
        for tap in range(taps.shape[1]):
            at = start - taps.shape[1] + 1 + tap
            weight = taps[part, tap : tap + 1, j * LANES : (j + 1) * LANES]
            term = weight * pad[first + j, at : at + rows, :]
            total = term if total is None else total + term
        out.append(total.astype(BF16))
    return jnp.concatenate(out, 1)


def features(part, diag, ones, heads, together):
    rows, width = part.shape[0], part.shape[1] // heads
    feat, share = diag.shape[1] // heads, ones.shape[1] // heads
    part_f = part.astype(F32)
    out = []
    for first in range(0, heads, together):
        at = slice(first * width, (first + together) * width)
        logits = dot(part[:, at], diag[at, first * feat : (first + together) * feat])
        squares = dot((part_f[:, at] * part_f[:, at]).astype(BF16), ones[at, :])
        scale = lax.rsqrt(squares * (1.0 / width) + EPS) * (LOG2E / math.sqrt(width))
        for k in range(together):
            lane = (first + k) * share
            mine = jnp.broadcast_to(scale[:, lane : lane + 1], (rows, feat))
            out.append(jnp.exp2(logits[:, k * feat : (k + 1) * feat] * mine).astype(BF16))
    return jnp.concatenate(out, 1)


def rim_rows(pad, nrim, weights, masks):
    keep = masks[1:2, : weights[0].shape[1]]
    c = 0
    for w in weights:
        proj = dot(nrim, w).astype(BF16).astype(F32) * keep
        for j in range(w.shape[1] // LANES):
            pad[c, 0:PAD, :] = proj[RIM - PAD :, j * LANES : (j + 1) * LANES]
            c += 1


def key_body(masks, normed, nrim, weight, taps, feat_w, kf, val, before, total, diag, ones, pad):
    heads, head_dim, feat = feat_w.shape
    cols = val.shape[1]
    tiles = cols // LANES
    diag[...] = jnp.zeros_like(diag)
    share = LANES // heads
    of_row = lax.broadcasted_iota(jnp.int32, ones.shape, 0) // head_dim
    of_col = lax.broadcasted_iota(jnp.int32, ones.shape, 1) // share
    ones[...] = jnp.where(of_row == of_col, 1.0, 0.0).astype(BF16)
    for h in range(heads):
        diag[h * head_dim : (h + 1) * head_dim, h * feat : (h + 1) * feat] = feat_w[h]
    weights = (weight[1], weight[2])
    total[...] = jnp.zeros_like(total)
    rows = normed.shape[0]
    store_proj(pad, normed[...], weights, PAD)
    rim_rows(pad, nrim(), weights, masks)
    key = convolve(pad, taps, 1, 0, tiles, PAD, rows)
    value = convolve(pad, taps, 2, tiles, tiles, PAD, rows)
    val[...] = value
    key_feat = features(key, diag, ones, heads, 2)
    kf[...] = key_feat
    for b in range(rows // SUB):
        sub = slice(b * SUB, (b + 1) * SUB)
        before[b] = total[...]
        for pair in range(heads // 2):
            vp = value[sub, pair * 2 * head_dim : (pair + 1) * 2 * head_dim]
            kp = key_feat[sub, pair * 2 * feat : (pair + 1) * 2 * feat]
            both = dot(vp, kp, TN)
            for side in range(2):
                h = pair * 2 + side
                total[h * head_dim : (h + 1) * head_dim, :] += both[
                    side * head_dim : (side + 1) * head_dim, side * feat : (side + 1) * feat
                ]
        sums = jnp.sum(key_feat[sub].astype(F32), 0, keepdims=True)
        for h in range(heads):
            at = heads * head_dim + h
            total[at : at + 1, :] += sums[:, h * feat : (h + 1) * feat]


def first_key_kernel(
    masks, far_rim, near_rim, ew_a, ew_b, gain, normed, weight, taps, feat_w,
    nrim, kf, val, before, total, diag, ones, pad,
):
    half = ew_a.shape[0]
    own = jnp.broadcast_to(masks[0:1, :], (RIM, half)) == 0
    far, near = far_rim[...].astype(F32), near_rim[...].astype(F32)
    rim = jnp.concatenate(
        [jnp.where(own, far[:, :half], near[:, :half]), jnp.where(own, far[:, half:], near[:, half:])],
        1,
    )
    lo, hi = rim[:, :half], rim[:, half:]
    mine = jnp.where(own, lo, hi).astype(BF16)
    other = jnp.where(own, hi, lo).astype(BF16)

    def rows_ahead():
        nrim[...] = normalize(dot(mine, ew_a[...]) + dot(other, ew_b[...]), gain[...])
        return nrim[...]

    key_body(masks, normed, rows_ahead, weight, taps, feat_w, kf, val, before, total, diag, ones, pad)


def key_kernel(
    masks, normed, nrim, weight, taps, feat_w, ow_hbm,
    kf, val, before, total, diag, ones, ow, pad, sem,
):
    copy = pltpu.make_async_copy(ow_hbm, ow, sem)
    copy.start()
    key_body(
        masks, normed, lambda: nrim[...], weight, taps, feat_w,
        kf, val, before, total, diag, ones, pad,
    )
    copy.wait()


def query_kernel(
    masks, after, normed, nrim, weight, taps, diag, ones, kf, val, qf, out, pad, *, heads
):
    del after
    rows = normed.shape[0]
    feat = qf.shape[1] // heads
    width = val.shape[1] // heads
    row = lax.broadcasted_iota(jnp.int32, (SUB, SUB), 0)
    col = lax.broadcasted_iota(jnp.int32, (SUB, SUB), 1)
    causal = row >= col
    left = (lax.broadcasted_iota(jnp.int32, (SUB, 4 * width), 1) & (2 * width - 1)) < width
    one = jnp.ones((SUB, 2 * width), BF16)
    rim_rows(pad, nrim[...], (weight[0],), masks)
    store_proj(pad, normed[...], (weight[0],), PAD)
    query = convolve(pad, taps, 0, 0, weight.shape[2] // LANES, PAD, rows)
    query_feat = features(query, diag, ones, heads, heads)
    qf[...] = query_feat
    for b in range(rows // SUB):
        sub = slice(b * SUB, (b + 1) * SUB)
        for pair in range(heads // 2):
            weights = []
            for h in (2 * pair, 2 * pair + 1):
                at = slice(h * feat, (h + 1) * feat)
                scores = dot(query_feat[sub, at], kf[sub, at], NT)
                weights.append(jnp.where(causal, scores, 0.0).astype(BF16))
            vp = val[sub, pair * 2 * width : (pair + 1) * 2 * width]
            both = dot(jnp.concatenate(weights, 0), jnp.concatenate([vp, one], 1))
            out[sub, pair * 4 * width : (pair + 1) * 4 * width] = jnp.where(
                left, both[:SUB], both[SUB:]
            )


def attend(qf, local, before, state_in, b, heads):
    feat = qf.shape[1] // heads
    width = local.shape[1] // heads // 2
    zero = jnp.zeros((width, feat), BF16)
    rows = slice(b * SUB, (b + 1) * SUB)
    state = (before[b] + state_in).astype(BF16)
    out = []
    for pair in range(heads // 2):
        h = pair * 2
        s0, s1 = (state[(h + k) * width : (h + k + 1) * width] for k in range(2))
        t0, t1 = (
            jnp.broadcast_to(
                state[heads * width + h + k : heads * width + h + k + 1], (width, feat)
            )
            for k in range(2)
        )
        rhs = jnp.concatenate(
            [
                jnp.concatenate([s0, zero], 1),
                jnp.concatenate([zero, s1], 1),
                jnp.concatenate([t0, zero], 1),
                jnp.concatenate([zero, t1], 1),
            ],
            0,
        )
        both = local[rows, pair * 4 * width : (pair + 1) * 4 * width] + dot(
            qf[rows, pair * 2 * feat : (pair + 1) * 2 * feat], rhs, NT
        )
        out.append((both[:, : 2 * width] / both[:, 2 * width :]).astype(BF16))
    return jnp.concatenate(out, 1)


def own_kernel(qf, local, before, state, weight, out, *, heads):
    attended = [
        attend(qf, local, before, state[...], b, heads) for b in range(qf.shape[0] // SUB)
    ]
    out[...] = dot(jnp.concatenate(attended, 0), weight[...])


def last_kernel(qf, local, before, state, weight, partial, out, buf, sem, *, heads):
    copies = []
    state_in = state[...].astype(F32)
    per = buf.shape[1] // SUB
    for s in range(buf.shape[0]):
        attended = [
            attend(qf, local, before, state_in, s * per + b, heads) for b in range(per)
        ]
        rows = slice(s * per * SUB, (s + 1) * per * SUB)
        buf[s] = (partial[rows, :] + dot(jnp.concatenate(attended, 0), weight[...])).astype(BF16)
        copies.append(
            pltpu.make_async_copy(buf.at[s], out.at[pl.ds(s * per * SUB, per * SUB), :], sem.at[s])
        )
        copies[-1].start()
    for copy in copies:
        copy.wait()


def swap(array, axis, by):
    devices = lax.axis_size(axis)
    return lax.ppermute(array, axis, [(i, i ^ by) for i in range(devices)])


def rounds(axis):
    devices, span, out = lax.axis_size(axis), 1, []
    while span < devices:
        radix = min(4, devices // span)
        out.append((span, radix))
        span *= radix
    return out


def earlier(axis):
    place = lax.axis_index(axis)
    flags = []
    for span, radix in rounds(axis):
        digit = (place >> (span.bit_length() - 1)) & (radix - 1)
        flags += [(digit ^ k) < digit for k in range(1, radix)]
    return flags


def prefix(group, axis, masks, covers):
    near = jnp.zeros(group.shape, F32)
    row = 0
    for span, radix in rounds(axis):
        sent = group.astype(BF16)
        if covers:
            covers.pop(0)(sent)
        for k in range(radix - 1, 0, -1):
            got = swap(sent, axis, k * span).astype(F32)
            group = group + got
            near = near + jnp.where(masks[row + k - 1 : row + k] > 0, got, 0.0)
        row += radix - 1
    while covers:
        covers.pop(0)(group)
    return near


def shards(signal, embed_weight, norm_gain, qkv_weight, conv_weight, feature_weight, out_weight):
    rows, depth = signal.shape
    rows //= 2
    half, width = embed_weight.shape
    cols = qkv_weight.shape[2]
    heads, head_dim, feat = feature_weight.shape
    feats = heads * feat
    states = heads * head_dim + 16
    blocks = rows // SUB
    place, rep = lax.axis_index("tm"), lax.axis_index("rep")
    devices = lax.axis_size("tm")
    hbm = pltpu.HBM

    flags = jnp.stack([rep > 0, 2 * place + rep > 0, *earlier("tm")]).astype(F32)
    masks = jnp.broadcast_to(flags[:, None], (flags.size, half))
    masks, signal, embed_weight, norm_gain, qkv_weight, conv_weight, feature_weight = (
        lax.optimization_barrier(
            (masks, signal, embed_weight, norm_gain, qkv_weight, conv_weight, feature_weight)
        )
    )
    second = masks[:1, :feat] > 0
    ew_other = swap(embed_weight, "rep", 1)
    (far_rim,) = call(
        rim_kernel,
        [(masks, None), (signal, hbm)],
        [((RIM, depth), BF16, None)],
        "rim",
        [pltpu.SemaphoreType.DMA],
        (1 << 30, 1 << 20),
    )
    ring = [(2 * i, 2 * i + 2) for i in range(devices - 1)] + [(2 * devices - 2, 2 * devices - 1)]
    ring += [(2 * i + 1, 2 * i - 1) for i in range(1, devices)] + [(1, 0)]
    far_rim = lax.ppermute(far_rim, ("tm", "rep"), ring)
    wqkv = [qkv_weight.transpose(1, 0, 2), swap(qkv_weight.transpose(1, 0, 2), "rep", 1)]
    taps = [conv_weight.transpose(1, 0, 2), swap(conv_weight.transpose(1, 0, 2), "rep", 1)]
    feat_w = [feature_weight, swap(feature_weight, "rep", 1)]
    gain = norm_gain.reshape(1, width)

    normed, near_rim = call(
        embed_kernel,
        vmem(signal, embed_weight, ew_other, gain),
        [((rows, width), BF16, None), ((RIM, depth), BF16, None)],
        "embed",
        (),
        (2 * rows * depth * width, 4 << 20),
    )

    key_outs = [
        ((rows, feats), BF16, None),
        ((rows, cols), BF16, None),
        ((blocks, states, feat), F32, None),
        ((states, feat), F32, None),
        ((cols, feats), BF16, None),
        ((cols, LANES), BF16, None),
    ]
    pads = pltpu.VMEM((2 * cols // LANES, PAD + rows, LANES), F32)
    key_work = (6 * rows * width * 2 * cols, 4 << 20)
    nrim, *other = call(
        first_key_kernel,
        [
            *vmem(masks, far_rim, near_rim, embed_weight, ew_other, gain, normed),
            *vmem(wqkv[1], taps[1], feat_w[1]),
        ],
        [((RIM, width), BF16, None), *key_outs],
        "keys_other",
        [pads],
        key_work,
    )
    back = swap(other[3].astype(BF16), "rep", 1).astype(F32)
    own = call(
        key_kernel,
        [*vmem(masks, normed, nrim, wqkv[0], taps[0], feat_w[0]), (out_weight, hbm)],
        [*key_outs, (out_weight.shape, BF16, None)],
        "keys_own",
        [pads, pltpu.SemaphoreType.DMA],
        key_work,
    )
    qf, local, ow = [None] * 2, [None] * 2, [own[6]]

    def query(k, keys, after):
        qf[k], local[k] = call(
            functools.partial(query_kernel, heads=heads),
            vmem(masks, after, normed, nrim, wqkv[k], taps[k], *keys[4:6], *keys[:2]),
            [((rows, feats), BF16, None), ((rows, 2 * cols), F32, None)],
            "queries",
            [pltpu.VMEM((cols // LANES, PAD + rows, LANES), F32)],
            (6 * rows * width * cols, 4 << 20),
        )
        if k == 1:
            ow.append(swap(lax.optimization_barrier((ow[0], after))[0], "rep", 1))

    covers = [functools.partial(query, 0, own), functools.partial(query, 1, other)]
    before = prefix(own[3] + back, "tm", masks[2:, :feat], covers)
    state_own = before + jnp.where(second, back, 0.0)
    state_other = swap((before + jnp.where(second, 0.0, own[3])).astype(BF16), "rep", 1)

    (partial,) = call(
        functools.partial(own_kernel, heads=heads),
        vmem(qf[0], local[0], own[2], state_own, ow[0]),
        [((rows, width), F32, None)],
        "attend_own",
        (),
        (4 * rows * width * cols, 4 << 20),
    )
    return call(
        functools.partial(last_kernel, heads=heads),
        vmem(qf[1], local[1], other[2], state_other, ow[1], partial),
        [((rows, width), BF16, hbm)],
        "attend_other",
        [pltpu.VMEM((2, rows // 2, width), BF16), pltpu.SemaphoreType.DMA((2,))],
        (4 * rows * width * cols, 4 << 20),
    )[0]


def solution(mesh):
    in_specs = (
        P(("groups", "tm"), None),
        P("rep", None),
        P(),
        P(None, None, "rep"),
        P(None, None, "rep"),
        P("rep", None, None),
        P("rep", None),
    )
    out_specs = P(("groups", "tm", "rep"), None)
    return jax.shard_map(shards, mesh=mesh, in_specs=in_specs, out_specs=out_specs, check_vma=False)
```

```python
import functools
import math

import jax
import jax.numpy as jnp
from jax import lax
from jax.experimental import pallas as pl
from jax.experimental.pallas import tpu as pltpu
from jax.sharding import PartitionSpec as P

EPS = 1e-05
LOG2E = math.log2(math.e)
SUB = 256
STEP = 512
RIM = 16
PAD = 8
LANES = 128
TILE = 8
F32 = jnp.float32
BF16 = jnp.bfloat16
NN = (((1,), (0,)), ((), ()))
NT = (((1,), (1,)), ((), ()))
TN = (((0,), (0,)), ((), ()))


def dot(a, b, dims=NN):
    return lax.dot_general(a, b, dims, preferred_element_type=F32)


def call(kernel, ins, outs, name, scratch=(), work=(1, 1), mib=16):
    def spec(place):
        return pl.BlockSpec(memory_space=pltpu.VMEM if place is None else place)

    def pinned(array, place):
        return pltpu.with_memory_space_constraint(array, place) if place is pltpu.HBM else array

    return pl.pallas_call(
        kernel,
        in_specs=[spec(p) for _, p in ins],
        out_specs=[spec(p) for _, _, p in outs],
        out_shape=[jax.ShapeDtypeStruct(s, t) for s, t, _ in outs],
        scratch_shapes=list(scratch),
        compiler_params=pltpu.CompilerParams(vmem_limit_bytes=mib << 20),
        cost_estimate=pl.CostEstimate(flops=work[0] << 3, bytes_accessed=work[1], transcendentals=0),
        name=name,
    )(*[pinned(*i) for i in ins])


def vmem(*arrays):
    return [(a, None) for a in arrays]


def normalize(emb, gain):
    mean = jnp.mean(emb * emb, -1, keepdims=True)
    return (emb * lax.rsqrt(mean + EPS) * gain).astype(BF16)


def rim_kernel(after, sig, feat_hbm, taps_hbm, rim, small, feat_w, taps, sem):
    del after
    copies = [
        pltpu.make_async_copy(sig.at[pl.ds(sig.shape[0] - RIM, RIM), :], rim, sem.at[0]),
        pltpu.make_async_copy(feat_hbm, feat_w, sem.at[1]),
        pltpu.make_async_copy(taps_hbm, taps, sem.at[2]),
    ]
    for copy in copies:
        copy.start()
    for copy in copies:
        copy.wait()
    heads, head_dim, _ = feat_w.shape
    for h in range(heads):
        small[h * head_dim : (h + 1) * head_dim, :] = feat_w[h].astype(F32)
    parts, count, cols = taps.shape
    small[heads * head_dim :, :] = jnp.zeros((small.shape[0] - heads * head_dim, LANES), F32)
    for part in range(parts):
        for j in range(cols // LANES):
            at = heads * head_dim + TILE * (part * (cols // LANES) + j)
            small[at : at + count, :] = taps[part, :, j * LANES : (j + 1) * LANES]


def embed_kernel(sig, ew_a, ew_b, gain, normed, near_rim):
    rep = lax.axis_index("rep")
    rows = normed.shape[0]
    half = ew_a.shape[0]
    own = pl.ds(pl.multiple_of(rep * half, half), half)
    other = pl.ds(pl.multiple_of((1 - rep) * half, half), half)
    near_rim[...] = sig[rows - RIM : rows, :]
    for b in range(rows // STEP):
        at = pl.ds(pl.multiple_of(rep * rows + b * STEP, STEP), STEP)
        normed[b * STEP : (b + 1) * STEP, :] = normalize(
            dot(sig[at, own], ew_a[...]) + dot(sig[at, other], ew_b[...]), gain[...]
        )


def store_proj(pad, normed, weights, start):
    rows = normed.shape[0]
    c = 0
    for w in weights:
        proj = dot(normed, w).astype(BF16).astype(F32)
        for j in range(w.shape[1] // LANES):
            pad[c, start : start + rows, :] = proj[:, j * LANES : (j + 1) * LANES]
            c += 1


def convolve(pad, small, dims, part, first, count, start, rows):
    heads, head_dim, _, taps = dims
    out = []
    for j in range(count):
        total = None
        row = heads * head_dim + TILE * (part * count + j)
        for tap in range(taps):
            at = start - taps + 1 + tap
            term = small[row + tap : row + tap + 1, :] * pad[first + j, at : at + rows, :]
            total = term if total is None else total + term
        out.append(total.astype(BF16))
    return jnp.concatenate(out, 1)


def features(part, diag, ones, heads, together):
    rows, width = part.shape[0], part.shape[1] // heads
    feat, share = diag.shape[1] // heads, ones.shape[1] // heads
    part_f = part.astype(F32)
    out = []
    for first in range(0, heads, together):
        at = slice(first * width, (first + together) * width)
        logits = dot(part[:, at], diag[at, first * feat : (first + together) * feat])
        squares = dot((part_f[:, at] * part_f[:, at]).astype(BF16), ones[at, :])
        scale = lax.rsqrt(squares * (1.0 / width) + EPS) * (LOG2E / math.sqrt(width))
        for k in range(together):
            lane = (first + k) * share
            mine = jnp.broadcast_to(scale[:, lane : lane + 1], (rows, feat))
            out.append(jnp.exp2(logits[:, k * feat : (k + 1) * feat] * mine).astype(BF16))
    return jnp.concatenate(out, 1)


def rim_rows(pad, nrim, weights, masks):
    keep = masks[1:2, : weights[0].shape[1]]
    c = 0
    for w in weights:
        proj = dot(nrim, w).astype(BF16).astype(F32) * keep
        for j in range(w.shape[1] // LANES):
            pad[c, 0:PAD, :] = proj[RIM - PAD :, j * LANES : (j + 1) * LANES]
            c += 1


def key_body(masks, normed, nrim, weight, small, kf, val, before, total, diag, ones, pad, dims):
    heads, head_dim, feat, _ = dims
    cols = val.shape[1]
    tiles = cols // LANES
    diag[...] = jnp.zeros_like(diag)
    share = LANES // heads
    of_row = lax.broadcasted_iota(jnp.int32, ones.shape, 0) // head_dim
    of_col = lax.broadcasted_iota(jnp.int32, ones.shape, 1) // share
    ones[...] = jnp.where(of_row == of_col, 1.0, 0.0).astype(BF16)
    for h in range(heads):
        here = slice(h * head_dim, (h + 1) * head_dim)
        diag[here, h * feat : (h + 1) * feat] = small[here, :].astype(BF16)
    weights = (weight[1], weight[2])
    total[...] = jnp.zeros_like(total)
    rows = normed.shape[0]
    store_proj(pad, normed[...], weights, PAD)
    rim_rows(pad, nrim(), weights, masks)
    key = convolve(pad, small, dims, 1, 0, tiles, PAD, rows)
    value = convolve(pad, small, dims, 2, tiles, tiles, PAD, rows)
    val[...] = value
    key_feat = features(key, diag, ones, heads, 2)
    kf[...] = key_feat
    for b in range(rows // SUB):
        sub = slice(b * SUB, (b + 1) * SUB)
        before[b] = total[...]
        for pair in range(heads // 2):
            vp = value[sub, pair * 2 * head_dim : (pair + 1) * 2 * head_dim]
            kp = key_feat[sub, pair * 2 * feat : (pair + 1) * 2 * feat]
            both = dot(vp, kp, TN)
            for side in range(2):
                h = pair * 2 + side
                total[h * head_dim : (h + 1) * head_dim, :] += both[
                    side * head_dim : (side + 1) * head_dim, side * feat : (side + 1) * feat
                ]
        sums = jnp.sum(key_feat[sub].astype(F32), 0, keepdims=True)
        for h in range(heads):
            at = heads * head_dim + h
            total[at : at + 1, :] += sums[:, h * feat : (h + 1) * feat]


def first_key_kernel(
    masks, far_rim, near_rim, ew_a, ew_b, gain, normed, weight, small,
    nrim, kf, val, before, total, diag, ones, pad, *, dims,
):
    half = ew_a.shape[0]
    own = jnp.broadcast_to(masks[0:1, :], (RIM, half)) == 0
    far, near = far_rim[...].astype(F32), near_rim[...].astype(F32)
    rim = jnp.concatenate(
        [jnp.where(own, far[:, :half], near[:, :half]), jnp.where(own, far[:, half:], near[:, half:])],
        1,
    )
    lo, hi = rim[:, :half], rim[:, half:]
    mine = jnp.where(own, lo, hi).astype(BF16)
    other = jnp.where(own, hi, lo).astype(BF16)

    def rows_ahead():
        nrim[...] = normalize(dot(mine, ew_a[...]) + dot(other, ew_b[...]), gain[...])
        return nrim[...]

    key_body(
        masks, normed, rows_ahead, weight, small, kf, val, before, total, diag, ones, pad, dims
    )


def key_kernel(
    masks, normed, nrim, weight, small, ow_hbm,
    kf, val, before, total, diag, ones, ow, pad, sem, *, dims,
):
    copy = pltpu.make_async_copy(ow_hbm, ow, sem)
    copy.start()
    key_body(
        masks, normed, lambda: nrim[...], weight, small,
        kf, val, before, total, diag, ones, pad, dims,
    )
    copy.wait()


def query_kernel(
    masks, after, normed, nrim, weight, small, diag, ones, kf, val, qf, out, pad, *, dims
):
    del after
    rows = normed.shape[0]
    heads, width, feat, _ = dims
    row = lax.broadcasted_iota(jnp.int32, (SUB, SUB), 0)
    col = lax.broadcasted_iota(jnp.int32, (SUB, SUB), 1)
    causal = row >= col
    left = (lax.broadcasted_iota(jnp.int32, (SUB, 4 * width), 1) & (2 * width - 1)) < width
    one = jnp.ones((SUB, 2 * width), BF16)
    rim_rows(pad, nrim[...], (weight[0],), masks)
    store_proj(pad, normed[...], (weight[0],), PAD)
    query = convolve(pad, small, dims, 0, 0, weight.shape[2] // LANES, PAD, rows)
    query_feat = features(query, diag, ones, heads, heads)
    qf[...] = query_feat
    for b in range(rows // SUB):
        sub = slice(b * SUB, (b + 1) * SUB)
        for pair in range(heads // 2):
            weights = []
            for h in (2 * pair, 2 * pair + 1):
                at = slice(h * feat, (h + 1) * feat)
                scores = dot(query_feat[sub, at], kf[sub, at], NT)
                weights.append(jnp.where(causal, scores, 0.0).astype(BF16))
            vp = val[sub, pair * 2 * width : (pair + 1) * 2 * width]
            both = dot(jnp.concatenate(weights, 0), jnp.concatenate([vp, one], 1))
            out[sub, pair * 4 * width : (pair + 1) * 4 * width] = jnp.where(
                left, both[:SUB], both[SUB:]
            )


def attend(qf, local, before, state_in, b, heads):
    feat = qf.shape[1] // heads
    width = local.shape[1] // heads // 2
    zero = jnp.zeros((width, feat), BF16)
    rows = slice(b * SUB, (b + 1) * SUB)
    state = (before[b] + state_in).astype(BF16)
    out = []
    for pair in range(heads // 2):
        h = pair * 2
        s0, s1 = (state[(h + k) * width : (h + k + 1) * width] for k in range(2))
        t0, t1 = (
            jnp.broadcast_to(
                state[heads * width + h + k : heads * width + h + k + 1], (width, feat)
            )
            for k in range(2)
        )
        rhs = jnp.concatenate(
            [
                jnp.concatenate([s0, zero], 1),
                jnp.concatenate([zero, s1], 1),
                jnp.concatenate([t0, zero], 1),
                jnp.concatenate([zero, t1], 1),
            ],
            0,
        )
        both = local[rows, pair * 4 * width : (pair + 1) * 4 * width] + dot(
            qf[rows, pair * 2 * feat : (pair + 1) * 2 * feat], rhs, NT
        )
        out.append((both[:, : 2 * width] / both[:, 2 * width :]).astype(BF16))
    return jnp.concatenate(out, 1)


def own_kernel(qf, local, before, state, weight, out, *, heads):
    attended = [
        attend(qf, local, before, state[...], b, heads) for b in range(qf.shape[0] // SUB)
    ]
    out[...] = dot(jnp.concatenate(attended, 0), weight[...])


def last_kernel(qf, local, before, state, weight, partial, out, buf, sem, *, heads):
    copies = []
    state_in = state[...].astype(F32)
    per = buf.shape[1] // SUB
    for s in range(buf.shape[0]):
        attended = [
            attend(qf, local, before, state_in, s * per + b, heads) for b in range(per)
        ]
        rows = slice(s * per * SUB, (s + 1) * per * SUB)
        buf[s] = (partial[rows, :] + dot(jnp.concatenate(attended, 0), weight[...])).astype(BF16)
        copies.append(
            pltpu.make_async_copy(buf.at[s], out.at[pl.ds(s * per * SUB, per * SUB), :], sem.at[s])
        )
        copies[-1].start()
    for copy in copies:
        copy.wait()


def swap(array, axis, by):
    devices = lax.axis_size(axis)
    return lax.ppermute(array, axis, [(i, i ^ by) for i in range(devices)])


def rounds(axis):
    devices, span, out = lax.axis_size(axis), 1, []
    while span < devices:
        radix = min(4, devices // span)
        out.append((span, radix))
        span *= radix
    return out


def earlier(axis):
    place = lax.axis_index(axis)
    flags = []
    for span, radix in rounds(axis):
        digit = (place >> (span.bit_length() - 1)) & (radix - 1)
        flags += [(digit ^ k) < digit for k in range(1, radix)]
    return flags


def prefix(group, axis, masks, covers):
    near = jnp.zeros(group.shape, F32)
    row = 0
    for span, radix in rounds(axis):
        sent = group.astype(BF16)
        if covers:
            covers.pop(0)(sent)
        for k in range(radix - 1, 0, -1):
            got = swap(sent, axis, k * span).astype(F32)
            group = group + got
            near = near + jnp.where(masks[row + k - 1 : row + k] > 0, got, 0.0)
        row += radix - 1
    while covers:
        covers.pop(0)(group)
    return near


def shards(signal, embed_weight, norm_gain, qkv_weight, conv_weight, feature_weight, out_weight):
    rows, depth = signal.shape
    rows //= 2
    half, width = embed_weight.shape
    cols = qkv_weight.shape[2]
    heads, head_dim, feat = feature_weight.shape
    feats = heads * feat
    states = heads * head_dim + 16
    blocks = rows // SUB
    place, rep = lax.axis_index("tm"), lax.axis_index("rep")
    devices = lax.axis_size("tm")
    hbm = pltpu.HBM

    flags = jnp.stack([rep > 0, 2 * place + rep > 0, *earlier("tm")]).astype(F32)
    masks = jnp.broadcast_to(flags[:, None], (flags.size, half))
    masks, signal, embed_weight, norm_gain, qkv_weight, conv_weight, feature_weight = (
        lax.optimization_barrier(
            (masks, signal, embed_weight, norm_gain, qkv_weight, conv_weight, feature_weight)
        )
    )
    second = masks[:1, :feat] > 0
    ew_other = swap(embed_weight, "rep", 1)
    conv_parts = conv_weight.transpose(1, 0, 2)
    small_rows = heads * head_dim + TILE * conv_parts.shape[0] * (cols // LANES)
    far_rim, small_own = call(
        rim_kernel,
        [(masks, None), (signal, hbm), (feature_weight, hbm), (conv_parts, hbm)],
        [((RIM, depth), BF16, None), ((small_rows, LANES), F32, None)],
        "rim",
        [
            pltpu.VMEM(feature_weight.shape, BF16),
            pltpu.VMEM(conv_parts.shape, F32),
            pltpu.SemaphoreType.DMA((3,)),
        ],
        (1 << 30, 1 << 20),
    )
    ring = [(2 * i, 2 * i + 2) for i in range(devices - 1)] + [(2 * devices - 2, 2 * devices - 1)]
    ring += [(2 * i + 1, 2 * i - 1) for i in range(1, devices)] + [(1, 0)]
    far_rim = lax.ppermute(far_rim, ("tm", "rep"), ring)
    wqkv = [qkv_weight.transpose(1, 0, 2), swap(qkv_weight.transpose(1, 0, 2), "rep", 1)]
    small = [small_own, swap(lax.optimization_barrier((small_own, ew_other))[0], "rep", 1)]
    dims = (heads, head_dim, feat, conv_weight.shape[0])
    gain = norm_gain.reshape(1, width)

    normed, near_rim = call(
        embed_kernel,
        vmem(signal, embed_weight, ew_other, gain),
        [((rows, width), BF16, None), ((RIM, depth), BF16, None)],
        "embed",
        (),
        (2 * rows * depth * width, 4 << 20),
    )

    key_outs = [
        ((rows, feats), BF16, None),
        ((rows, cols), BF16, None),
        ((blocks, states, feat), F32, None),
        ((states, feat), F32, None),
        ((cols, feats), BF16, None),
        ((cols, LANES), BF16, None),
    ]
    pads = pltpu.VMEM((2 * cols // LANES, PAD + rows, LANES), F32)
    key_work = (6 * rows * width * 2 * cols, 4 << 20)
    nrim, *other = call(
        functools.partial(first_key_kernel, dims=dims),
        [
            *vmem(masks, far_rim, near_rim, embed_weight, ew_other, gain, normed),
            *vmem(wqkv[1], small[1]),
        ],
        [((RIM, width), BF16, None), *key_outs],
        "keys_other",
        [pads],
        key_work,
    )
    back = swap(other[3].astype(BF16), "rep", 1).astype(F32)
    own = call(
        functools.partial(key_kernel, dims=dims),
        [*vmem(masks, normed, nrim, wqkv[0], small[0]), (out_weight, hbm)],
        [*key_outs, (out_weight.shape, BF16, None)],
        "keys_own",
        [pads, pltpu.SemaphoreType.DMA],
        key_work,
    )
    qf, local, ow = [None] * 2, [None] * 2, [own[6]]

    def query(k, keys, after):
        qf[k], local[k] = call(
            functools.partial(query_kernel, dims=dims),
            vmem(masks, after, normed, nrim, wqkv[k], small[k], *keys[4:6], *keys[:2]),
            [((rows, feats), BF16, None), ((rows, 2 * cols), F32, None)],
            "queries",
            [pltpu.VMEM((cols // LANES, PAD + rows, LANES), F32)],
            (6 * rows * width * cols, 4 << 20),
        )
        if k == 1:
            ow.append(swap(lax.optimization_barrier((ow[0], after))[0], "rep", 1))

    covers = [functools.partial(query, 0, own), functools.partial(query, 1, other)]
    before = prefix(own[3] + back, "tm", masks[2:, :feat], covers)
    state_own = before + jnp.where(second, back, 0.0)
    state_other = swap((before + jnp.where(second, 0.0, own[3])).astype(BF16), "rep", 1)

    (partial,) = call(
        functools.partial(own_kernel, heads=heads),
        vmem(qf[0], local[0], own[2], state_own, ow[0]),
        [((rows, width), F32, None)],
        "attend_own",
        (),
        (4 * rows * width * cols, 4 << 20),
    )
    return call(
        functools.partial(last_kernel, heads=heads),
        vmem(qf[1], local[1], other[2], state_other, ow[1], partial),
        [((rows, width), BF16, hbm)],
        "attend_other",
        [pltpu.VMEM((2, rows // 2, width), BF16), pltpu.SemaphoreType.DMA((2,))],
        (4 * rows * width * cols, 4 << 20),
    )[0]


def solution(mesh):
    in_specs = (
        P(("groups", "tm"), None),
        P("rep", None),
        P(),
        P(None, None, "rep"),
        P(None, None, "rep"),
        P("rep", None, None),
        P("rep", None),
    )
    out_specs = P(("groups", "tm", "rep"), None)
    return jax.shard_map(shards, mesh=mesh, in_specs=in_specs, out_specs=out_specs, check_vma=False)
```

```python
import functools
import math

import jax
import jax.numpy as jnp
from jax import lax
from jax.experimental import pallas as pl
from jax.experimental.pallas import tpu as pltpu
from jax.sharding import PartitionSpec as P

EPS = 1e-05
LOG2E = math.log2(math.e)
SUB = 256
STEP = 512
RIM = 16
PAD = 8
LANES = 128
F32 = jnp.float32
BF16 = jnp.bfloat16
NN = (((1,), (0,)), ((), ()))
NT = (((1,), (1,)), ((), ()))
TN = (((0,), (0,)), ((), ()))


def dot(a, b, dims=NN):
    return lax.dot_general(a, b, dims, preferred_element_type=F32)


def call(kernel, ins, outs, name, scratch=(), work=(1, 1), mib=16):
    def spec(place):
        return pl.BlockSpec(memory_space=pltpu.VMEM if place is None else place)

    def pinned(array, place):
        return pltpu.with_memory_space_constraint(array, place) if place is pltpu.HBM else array

    return pl.pallas_call(
        kernel,
        in_specs=[spec(p) for _, p in ins],
        out_specs=[spec(p) for _, _, p in outs],
        out_shape=[jax.ShapeDtypeStruct(s, t) for s, t, _ in outs],
        scratch_shapes=list(scratch),
        compiler_params=pltpu.CompilerParams(vmem_limit_bytes=mib << 20),
        cost_estimate=pl.CostEstimate(flops=work[0] << 3, bytes_accessed=work[1], transcendentals=0),
        name=name,
    )(*[pinned(*i) for i in ins])


def vmem(*arrays):
    return [(a, None) for a in arrays]


def normalize(emb, gain):
    mean = jnp.mean(emb * emb, -1, keepdims=True)
    return (emb * lax.rsqrt(mean + EPS) * gain).astype(BF16)


def rim_kernel(after, sig, rim, sem):
    del after
    copy = pltpu.make_async_copy(sig.at[pl.ds(sig.shape[0] - RIM, RIM), :], rim, sem)
    copy.start()
    copy.wait()


def embed_kernel(sig, ew_a, ew_b, gain, normed, near_rim):
    rep = lax.axis_index("rep")
    rows = normed.shape[0]
    half = ew_a.shape[0]
    own = pl.ds(pl.multiple_of(rep * half, half), half)
    other = pl.ds(pl.multiple_of((1 - rep) * half, half), half)
    near_rim[...] = sig[rows - RIM : rows, :]
    for b in range(rows // STEP):
        at = pl.ds(pl.multiple_of(rep * rows + b * STEP, STEP), STEP)
        normed[b * STEP : (b + 1) * STEP, :] = normalize(
            dot(sig[at, own], ew_a[...]) + dot(sig[at, other], ew_b[...]), gain[...]
        )


def store_proj(pad, normed, weights, start):
    rows = normed.shape[0]
    c = 0
    for w in weights:
        proj = dot(normed, w).astype(BF16).astype(F32)
        for j in range(w.shape[1] // LANES):
            pad[c, start : start + rows, :] = proj[:, j * LANES : (j + 1) * LANES]
            c += 1


def convolve(pad, taps, part, first, count, start, rows):
    out = []
    for j in range(count):
        total = None
        for tap in range(taps.shape[1]):
            at = start - taps.shape[1] + 1 + tap
            weight = taps[part, tap : tap + 1, j * LANES : (j + 1) * LANES]
            term = weight * pad[first + j, at : at + rows, :]
            total = term if total is None else total + term
        out.append(total.astype(BF16))
    return jnp.concatenate(out, 1)


def features(part, diag, ones, heads, together):
    rows, width = part.shape[0], part.shape[1] // heads
    feat, share = diag.shape[1] // heads, ones.shape[1] // heads
    part_f = part.astype(F32)
    out = []
    for first in range(0, heads, together):
        at = slice(first * width, (first + together) * width)
        logits = dot(part[:, at], diag[at, first * feat : (first + together) * feat])
        squares = dot((part_f[:, at] * part_f[:, at]).astype(BF16), ones[at, :])
        scale = lax.rsqrt(squares * (1.0 / width) + EPS) * (LOG2E / math.sqrt(width))
        for k in range(together):
            lane = (first + k) * share
            mine = jnp.broadcast_to(scale[:, lane : lane + 1], (rows, feat))
            out.append(jnp.exp2(logits[:, k * feat : (k + 1) * feat] * mine).astype(BF16))
    return jnp.concatenate(out, 1)


def rim_rows(pad, nrim, weights, masks):
    keep = masks[1:2, : weights[0].shape[1]]
    c = 0
    for w in weights:
        proj = dot(nrim, w).astype(BF16).astype(F32) * keep
        for j in range(w.shape[1] // LANES):
            pad[c, 0:PAD, :] = proj[RIM - PAD :, j * LANES : (j + 1) * LANES]
            c += 1


def key_body(masks, normed, nrim, weight, taps, feat_w, kf, val, before, total, diag, ones, pad):
    heads, head_dim, feat = feat_w.shape
    cols = val.shape[1]
    tiles = cols // LANES
    diag[...] = jnp.zeros_like(diag)
    share = LANES // heads
    of_row = lax.broadcasted_iota(jnp.int32, ones.shape, 0) // head_dim
    of_col = lax.broadcasted_iota(jnp.int32, ones.shape, 1) // share
    ones[...] = jnp.where(of_row == of_col, 1.0, 0.0).astype(BF16)
    for h in range(heads):
        diag[h * head_dim : (h + 1) * head_dim, h * feat : (h + 1) * feat] = feat_w[h]
    weights = (weight[1], weight[2])
    total[...] = jnp.zeros_like(total)
    rows = normed.shape[0]
    store_proj(pad, normed[...], weights, PAD)
    rim_rows(pad, nrim(), weights, masks)
    key = convolve(pad, taps, 1, 0, tiles, PAD, rows)
    value = convolve(pad, taps, 2, tiles, tiles, PAD, rows)
    val[...] = value
    key_feat = features(key, diag, ones, heads, 2)
    kf[...] = key_feat
    for b in range(rows // SUB):
        sub = slice(b * SUB, (b + 1) * SUB)
        before[b] = total[...]
        for pair in range(heads // 2):
            vp = value[sub, pair * 2 * head_dim : (pair + 1) * 2 * head_dim]
            kp = key_feat[sub, pair * 2 * feat : (pair + 1) * 2 * feat]
            both = dot(vp, kp, TN)
            for side in range(2):
                h = pair * 2 + side
                total[h * head_dim : (h + 1) * head_dim, :] += both[
                    side * head_dim : (side + 1) * head_dim, side * feat : (side + 1) * feat
                ]
        sums = jnp.sum(key_feat[sub].astype(F32), 0, keepdims=True)
        for h in range(heads):
            at = heads * head_dim + h
            total[at : at + 1, :] += sums[:, h * feat : (h + 1) * feat]


def first_key_kernel(
    masks, far_rim, near_rim, ew_a, ew_b, gain, normed, weight, taps, feat_w,
    nrim, kf, val, before, total, diag, ones, pad,
):
    half = ew_a.shape[0]
    own = jnp.broadcast_to(masks[0:1, :], (RIM, half)) == 0
    far, near = far_rim[...].astype(F32), near_rim[...].astype(F32)
    rim = jnp.concatenate(
        [jnp.where(own, far[:, :half], near[:, :half]), jnp.where(own, far[:, half:], near[:, half:])],
        1,
    )
    lo, hi = rim[:, :half], rim[:, half:]
    mine = jnp.where(own, lo, hi).astype(BF16)
    other = jnp.where(own, hi, lo).astype(BF16)

    def rows_ahead():
        nrim[...] = normalize(dot(mine, ew_a[...]) + dot(other, ew_b[...]), gain[...])
        return nrim[...]

    key_body(masks, normed, rows_ahead, weight, taps, feat_w, kf, val, before, total, diag, ones, pad)


def key_kernel(
    masks, normed, nrim, weight, taps, feat_w, ow_hbm,
    kf, val, before, total, diag, ones, ow, pad, sem,
):
    copy = pltpu.make_async_copy(ow_hbm, ow, sem)
    copy.start()
    key_body(
        masks, normed, lambda: nrim[...], weight, taps, feat_w,
        kf, val, before, total, diag, ones, pad,
    )
    copy.wait()


def pair_rhs(state, pair, heads, width):
    feat = state.shape[1]
    zero = jnp.zeros((width, feat), BF16)
    rows = []
    for k in range(2):
        h = pair * 2 + k
        rows.append((state[h * width : (h + 1) * width], k))
    for k in range(2):
        at = heads * width + pair * 2 + k
        rows.append((jnp.broadcast_to(state[at : at + 1], (width, feat)), k))
    return jnp.concatenate(
        [jnp.concatenate([r, zero] if k == 0 else [zero, r], 1) for r, k in rows], 0
    )


def attend(qf, local, state, rows, heads):
    feat = qf.shape[1] // heads
    width = local.shape[1] // heads // 2
    out = []
    for pair in range(heads // 2):
        both = local[rows, pair * 4 * width : (pair + 1) * 4 * width] + dot(
            qf[rows, pair * 2 * feat : (pair + 1) * 2 * feat],
            pair_rhs(state, pair, heads, width),
            NT,
        )
        out.append((both[:, : 2 * width] / both[:, 2 * width :]).astype(BF16))
    return jnp.concatenate(out, 1)


def query_kernel(
    masks, after, normed, nrim, weight, taps, diag, ones, kf, val, before, qf, out, pad, *, heads
):
    del after
    rows = normed.shape[0]
    feat = qf.shape[1] // heads
    width = val.shape[1] // heads
    row = lax.broadcasted_iota(jnp.int32, (SUB, SUB), 0)
    col = lax.broadcasted_iota(jnp.int32, (SUB, SUB), 1)
    causal = row >= col
    left = (lax.broadcasted_iota(jnp.int32, (SUB, 4 * width), 1) & (2 * width - 1)) < width
    one = jnp.ones((SUB, 2 * width), BF16)
    rim_rows(pad, nrim[...], (weight[0],), masks)
    store_proj(pad, normed[...], (weight[0],), PAD)
    query = convolve(pad, taps, 0, 0, weight.shape[2] // LANES, PAD, rows)
    query_feat = features(query, diag, ones, heads, heads)
    qf[...] = query_feat
    for b in range(rows // SUB):
        sub = slice(b * SUB, (b + 1) * SUB)
        for pair in range(heads // 2):
            weights = []
            for h in (2 * pair, 2 * pair + 1):
                at = slice(h * feat, (h + 1) * feat)
                scores = dot(query_feat[sub, at], kf[sub, at], NT)
                weights.append(jnp.where(causal, scores, 0.0).astype(BF16))
            vp = val[sub, pair * 2 * width : (pair + 1) * 2 * width]
            both = dot(jnp.concatenate(weights, 0), jnp.concatenate([vp, one], 1))
            total = jnp.where(left, both[:SUB], both[SUB:])
            if b > 0:
                total = total + dot(
                    query_feat[sub, pair * 2 * feat : (pair + 1) * 2 * feat],
                    pair_rhs(before[b].astype(BF16), pair, heads, width),
                    NT,
                )
            out[sub, pair * 4 * width : (pair + 1) * 4 * width] = total


def own_kernel(qf, local, state, weight, out, *, heads):
    attended = attend(qf, local, state[...].astype(BF16), slice(None), heads)
    out[...] = dot(attended, weight[...])


def last_kernel(qf, local, state, weight, partial, out, buf, sem, *, heads):
    copies = []
    per = buf.shape[1]
    for s in range(buf.shape[0]):
        rows = slice(s * per, (s + 1) * per)
        attended = attend(qf, local, state[...], rows, heads)
        buf[s] = (partial[rows, :] + dot(attended, weight[...])).astype(BF16)
        copies.append(
            pltpu.make_async_copy(buf.at[s], out.at[pl.ds(s * per, per), :], sem.at[s])
        )
        copies[-1].start()
    for copy in copies:
        copy.wait()


def swap(array, axis, by):
    devices = lax.axis_size(axis)
    return lax.ppermute(array, axis, [(i, i ^ by) for i in range(devices)])


def rounds(axis):
    devices, span, out = lax.axis_size(axis), 1, []
    while span < devices:
        radix = min(4, devices // span)
        out.append((span, radix))
        span *= radix
    return out


def earlier(axis):
    place = lax.axis_index(axis)
    flags = []
    for span, radix in rounds(axis):
        digit = (place >> (span.bit_length() - 1)) & (radix - 1)
        flags += [(digit ^ k) < digit for k in range(1, radix)]
    return flags


def prefix(group, axis, masks, covers):
    near = jnp.zeros(group.shape, F32)
    row = 0
    for span, radix in rounds(axis):
        sent = group.astype(BF16)
        if covers:
            covers.pop(0)(sent)
        for k in range(radix - 1, 0, -1):
            got = swap(sent, axis, k * span).astype(F32)
            group = group + got
            near = near + jnp.where(masks[row + k - 1 : row + k] > 0, got, 0.0)
        row += radix - 1
    while covers:
        covers.pop(0)(group)
    return near


def shards(signal, embed_weight, norm_gain, qkv_weight, conv_weight, feature_weight, out_weight):
    rows, depth = signal.shape
    rows //= 2
    half, width = embed_weight.shape
    cols = qkv_weight.shape[2]
    heads, head_dim, feat = feature_weight.shape
    feats = heads * feat
    states = heads * head_dim + 16
    blocks = rows // SUB
    place, rep = lax.axis_index("tm"), lax.axis_index("rep")
    devices = lax.axis_size("tm")
    hbm = pltpu.HBM

    flags = jnp.stack([rep > 0, 2 * place + rep > 0, *earlier("tm")]).astype(F32)
    masks = jnp.broadcast_to(flags[:, None], (flags.size, half))
    masks, signal, embed_weight, norm_gain, qkv_weight, conv_weight, feature_weight = (
        lax.optimization_barrier(
            (masks, signal, embed_weight, norm_gain, qkv_weight, conv_weight, feature_weight)
        )
    )
    second = masks[:1, :feat] > 0
    ew_other = swap(embed_weight, "rep", 1)
    (far_rim,) = call(
        rim_kernel,
        [(masks, None), (signal, hbm)],
        [((RIM, depth), BF16, None)],
        "rim",
        [pltpu.SemaphoreType.DMA],
        (1 << 30, 1 << 20),
    )
    ring = [(2 * i, 2 * i + 2) for i in range(devices - 1)] + [(2 * devices - 2, 2 * devices - 1)]
    ring += [(2 * i + 1, 2 * i - 1) for i in range(1, devices)] + [(1, 0)]
    far_rim = lax.ppermute(far_rim, ("tm", "rep"), ring)
    wqkv = [qkv_weight.transpose(1, 0, 2), swap(qkv_weight.transpose(1, 0, 2), "rep", 1)]
    taps = [conv_weight.transpose(1, 0, 2), swap(conv_weight.transpose(1, 0, 2), "rep", 1)]
    feat_w = [feature_weight, swap(feature_weight, "rep", 1)]
    gain = norm_gain.reshape(1, width)

    normed, near_rim = call(
        embed_kernel,
        vmem(signal, embed_weight, ew_other, gain),
        [((rows, width), BF16, None), ((RIM, depth), BF16, None)],
        "embed",
        (),
        (2 * rows * depth * width, 4 << 20),
    )

    key_outs = [
        ((rows, feats), BF16, None),
        ((rows, cols), BF16, None),
        ((blocks, states, feat), F32, None),
        ((states, feat), F32, None),
        ((cols, feats), BF16, None),
        ((cols, LANES), BF16, None),
    ]
    pads = pltpu.VMEM((2 * cols // LANES, PAD + rows, LANES), F32)
    key_work = (6 * rows * width * 2 * cols, 4 << 20)
    nrim, *other = call(
        first_key_kernel,
        [
            *vmem(masks, far_rim, near_rim, embed_weight, ew_other, gain, normed),
            *vmem(wqkv[1], taps[1], feat_w[1]),
        ],
        [((RIM, width), BF16, None), *key_outs],
        "keys_other",
        [pads],
        key_work,
    )
    back = swap(other[3].astype(BF16), "rep", 1).astype(F32)
    own = call(
        key_kernel,
        [*vmem(masks, normed, nrim, wqkv[0], taps[0], feat_w[0]), (out_weight, hbm)],
        [*key_outs, (out_weight.shape, BF16, None)],
        "keys_own",
        [pads, pltpu.SemaphoreType.DMA],
        key_work,
    )
    qf, local, ow = [None] * 2, [None] * 2, [own[6]]

    def query(k, keys, after):
        qf[k], local[k] = call(
            functools.partial(query_kernel, heads=heads),
            vmem(masks, after, normed, nrim, wqkv[k], taps[k], *keys[4:6], *keys[:3]),
            [((rows, feats), BF16, None), ((rows, 2 * cols), F32, None)],
            "queries",
            [pltpu.VMEM((cols // LANES, PAD + rows, LANES), F32)],
            (6 * rows * width * cols, 4 << 20),
        )
        if k == 1:
            ow.append(swap(lax.optimization_barrier((ow[0], after))[0], "rep", 1))

    covers = [functools.partial(query, 0, own), functools.partial(query, 1, other)]
    before = prefix(own[3] + back, "tm", masks[2:, :feat], covers)
    state_own = before + jnp.where(second, back, 0.0)
    state_other = swap((before + jnp.where(second, 0.0, own[3])).astype(BF16), "rep", 1)

    (partial,) = call(
        functools.partial(own_kernel, heads=heads),
        vmem(qf[0], local[0], state_own, ow[0]),
        [((rows, width), F32, None)],
        "attend_own",
        (),
        (4 * rows * width * cols, 4 << 20),
    )
    return call(
        functools.partial(last_kernel, heads=heads),
        vmem(qf[1], local[1], state_other, ow[1], partial),
        [((rows, width), BF16, hbm)],
        "attend_other",
        [pltpu.VMEM((2, rows // 2, width), BF16), pltpu.SemaphoreType.DMA((2,))],
        (4 * rows * width * cols, 4 << 20),
    )[0]


def solution(mesh):
    in_specs = (
        P(("groups", "tm"), None),
        P("rep", None),
        P(),
        P(None, None, "rep"),
        P(None, None, "rep"),
        P("rep", None, None),
        P("rep", None),
    )
    out_specs = P(("groups", "tm", "rep"), None)
    return jax.shard_map(shards, mesh=mesh, in_specs=in_specs, out_specs=out_specs, check_vma=False)
```
